32 devices in a mesh: dp: 8 (over y, x, core), tensor: 4 (over z).
Axes of the slice: x: 2, y: 2, z: 4, core: 2. Of those that a mesh axis runs over, the one named last changes fastest.
Arguments:
- tokens: bfloat16 [2, 4096, 2048], P(None, ('dp', 'tensor')), may hold values from -6 to 6
- lengths: int32 [2, 8, 2], P(None, 'dp'), may hold values from 0 to 512, as said below
- mixer_gain: float32 [2048], replicated, may hold values from 0.5 to 1.5
- query_weight: bfloat16 [2048, 2048], P('dp', 'tensor'), may hold values from -0.125 to 0.125
- key_weight: bfloat16 [2048, 2048], P('dp', 'tensor'), may hold values from -0.125 to 0.125
- value_weight: bfloat16 [2048, 4096], P('dp', 'tensor'), may hold values from -0.125 to 0.125
- outgate_weight: bfloat16 [2048, 4096], P('dp', 'tensor'), may hold values from -0.125 to 0.125
- alpha_weight: bfloat16 [2048, 16], P('dp', 'tensor'), may hold values from -0.125 to 0.125
- beta_weight: bfloat16 [2048, 16], P('dp', 'tensor'), may hold values from -0.125 to 0.125
- query_conv: float32 [4, 2048], replicated, may hold values from -3 to 3
- key_conv: float32 [4, 2048], replicated, may hold values from -3 to 3
- value_conv: float32 [4, 4096], replicated, may hold values from -3 to 3
- log_rate: float32 [16], replicated, may hold values from -3 to 0
- rate_bias: float32 [16], replicated, may hold values from -5 to -2
- head_gain: float32 [256], replicated, may hold values from 0.5 to 1.5
- output_weight: bfloat16 [4096, 2048], P('tensor', 'dp'), may hold values from -0.125 to 0.125
- feed_gain: float32 [2048], replicated, may hold values from 0.5 to 1.5
- gate_weight: bfloat16 [2048, 5632], P('dp', 'tensor'), may hold values from -0.125 to 0.125
- up_weight: bfloat16 [2048, 5632], P('dp', 'tensor'), may hold values from -0.125 to 0.125
- down_weight: bfloat16 [5632, 2048], P('tensor', 'dp'), may hold values from -0.078125 to 0.078125
- cotangent: bfloat16 [2, 4096, 2048], P(None, ('dp', 'tensor')), may hold values from -6 to 6
Outputs:
- layer_out: bfloat16 [2, 4096, 2048], P(None, ('dp', 'tensor'))
- grad_tokens: float32 [2, 4096, 2048], P(None, ('dp', 'tensor'))
- grad_mixer_gain: float32 [2048], replicated
- grad_query_weight: float32 [2048, 2048], P('dp', 'tensor')
- grad_key_weight: float32 [2048, 2048], P('dp', 'tensor')
- grad_value_weight: float32 [2048, 4096], P('dp', 'tensor')
- grad_outgate_weight: float32 [2048, 4096], P('dp', 'tensor')
- grad_alpha_weight: float32 [2048, 16], P('dp', 'tensor')
- grad_beta_weight: float32 [2048, 16], P('dp', 'tensor')
- grad_query_conv: float32 [4, 2048], replicated
- grad_key_conv: float32 [4, 2048], replicated
- grad_value_conv: float32 [4, 4096], replicated
- grad_log_rate: float32 [16], replicated
- grad_rate_bias: float32 [16], replicated
- grad_head_gain: float32 [256], replicated
- grad_output_weight: float32 [4096, 2048], P('tensor', 'dp')
- grad_feed_gain: float32 [2048], replicated
- grad_gate_weight: float32 [2048, 5632], P('dp', 'tensor')
- grad_up_weight: float32 [2048, 5632], P('dp', 'tensor')
- grad_down_weight: float32 [5632, 2048], P('tensor', 'dp')
The draws below stay inside these ranges and needn't reach their ends.
Inputs may be any that keep to these rules, and one draw needn't show every extreme that they name: Each pair is the lengths of two sequences packed into 512 rows: the first starts at row 0 and has 256 to 512 rows; the second starts at the first length rounded up to a multiple of 64, has 0 or at least 256 rows and ends within 512; the pair of micro-batch 0 and data group 0 is (512, 0).
All inputs are finite; a program needn't handle non-finite values.
Results may differ from the reference program's by a relative error of at most 0.014.
Values may be sent and summed in bfloat16 or wider, within the bound.
No kernel may reach another device: no remote copies, remote signals or barrier semaphores. Data moves between devices by JAX's collectives and lax.ppermute only.
A program may use at most 384 MiB of HBM per device.

```python
import jax
import jax.numpy as jnp
from jax import lax

D = 2048
H = 16
DK = 128
DV = 256
FF = 5632
CONV = 4
STRETCH = 64
PACK = 512
LEAST = 256
MICRO = 2
TOKENS = 4096
N_DP = 8


def draw_lengths(key, part):
    first_key = jax.random.fold_in(key, 11)
    second_key = jax.random.fold_in(key, 23)
    first_len = jax.random.randint(first_key, (MICRO, N_DP), LEAST, PACK + 1)
    rounded = (first_len + STRETCH - 1) // STRETCH * STRETCH
    room = PACK - rounded
    raw_bits = jax.random.randint(second_key, (MICRO, N_DP), 0, 1 << 20)
    span_size = jnp.maximum(room - LEAST + 1, 1)
    second_len = jnp.where(room >= LEAST, LEAST + raw_bits % span_size, 0)
    first_len = first_len.at[0, 0].set(PACK)
    second_len = second_len.at[0, 0].set(0)
    return jnp.stack([first_len, second_len], axis=-1).astype(jnp.int32)


def level_of(own_key, extent, shards, least, high):
    def one(axis_at, shards_of):
        heights = jax.random.uniform(jax.random.fold_in(jax.random.fold_in(own_key, 6), axis_at), (shards_of,), jnp.float32, least / len(shards), high / len(shards))
        return jnp.repeat(jnp.exp(heights), extent[axis_at] // shards_of).reshape((-1,) + (1,) * (len(extent) - axis_at - 1))

    level = one(*shards[0])
    for cut in shards[1:]:
        level = level * one(*cut)
    return level


def noise(rng, dims, scale, most, shards=(), kind=jnp.bfloat16):
    drawn = scale * jax.random.normal(rng, dims, jnp.float32)
    if shards:
        drawn = drawn * level_of(rng, dims, shards, -0.22, 0.18)
    return jnp.clip(drawn, -most, most).astype(kind)


def setup_inputs(seed: int = 0) -> dict:
    key_list = jax.random.split(jax.random.key(seed), 22)
    tokens = noise(key_list[0], (MICRO, TOKENS, D), 1.0, 6.0, ((1, 32),))
    lengths = draw_lengths(jax.random.fold_in(key_list[21], 71), 0)
    mixer_gain = jnp.clip(1.0 + 0.1 * jax.random.normal(key_list[2], (D,), jnp.float32), 0.5, 1.5)
    query_weight = noise(key_list[3], (D, H * DK), D ** -0.5, 0.125, ((0, 8), (1, 4)))
    key_weight = noise(key_list[4], (D, H * DK), D ** -0.5, 0.125, ((0, 8), (1, 4)))
    value_weight = noise(key_list[5], (D, H * DV), D ** -0.5, 0.125, ((0, 8), (1, 4)))
    outgate_weight = noise(key_list[6], (D, H * DV), D ** -0.5, 0.125, ((0, 8), (1, 4)))
    alpha_weight = noise(key_list[7], (D, H), D ** -0.5, 0.125, ((0, 8), (1, 4)))
    beta_weight = noise(key_list[8], (D, H), D ** -0.5, 0.125, ((0, 8), (1, 4)))
    query_conv = noise(key_list[9], (CONV, H * DK), CONV ** -0.5, 3.0, (), jnp.float32)
    key_conv = noise(key_list[10], (CONV, H * DK), CONV ** -0.5, 3.0, (), jnp.float32)
    value_conv = noise(key_list[11], (CONV, H * DV), CONV ** -0.5, 3.0, (), jnp.float32)
    log_rate = jnp.clip(jax.random.uniform(key_list[12], (H,), jnp.float32, -3.0, 0.0), -3.0, 0.0)
    rate_bias = jnp.clip(jax.random.uniform(key_list[13], (H,), jnp.float32, -5.0, -2.0), -5.0, -2.0)
    head_gain = jnp.clip(1.0 + 0.1 * jax.random.normal(key_list[14], (DV,), jnp.float32), 0.5, 1.5)
    output_weight = noise(key_list[15], (H * DV, D), D ** -0.5, 0.125, ((0, 4), (1, 8)))
    feed_gain = jnp.clip(1.0 + 0.1 * jax.random.normal(key_list[16], (D,), jnp.float32), 0.5, 1.5)
    gate_weight = noise(key_list[17], (D, FF), D ** -0.5, 0.125, ((0, 8), (1, 4)))
    up_weight = noise(key_list[18], (D, FF), D ** -0.5, 0.125, ((0, 8), (1, 4)))
    down_weight = noise(key_list[19], (FF, D), FF ** -0.5, 0.078125, ((0, 4), (1, 8)))
    cotangent = noise(key_list[20], (MICRO, TOKENS, D), 1.0, 6.0, ((1, 32),))
    return dict(tokens=tokens, lengths=lengths, mixer_gain=mixer_gain, query_weight=query_weight, key_weight=key_weight, value_weight=value_weight, outgate_weight=outgate_weight, alpha_weight=alpha_weight, beta_weight=beta_weight, query_conv=query_conv, key_conv=key_conv, value_conv=value_conv, log_rate=log_rate, rate_bias=rate_bias, head_gain=head_gain, output_weight=output_weight, feed_gain=feed_gain, gate_weight=gate_weight, up_weight=up_weight, down_weight=down_weight, cotangent=cotangent)


precise = lax.Precision.HIGHEST

@jax.custom_vjp
def low(v):
    return lax.optimization_barrier(v.astype(jnp.bfloat16)).astype(jnp.float32)

@jax.custom_vjp
def low_back(v):
    return v

def low_keep(v):
    return (low(v), None)

def low_pass(kept, grad):
    return (grad,)

def back_keep(v):
    return (v, None)

def back_low(kept, grad):
    return (low(grad),)
low.defvjp(low_keep, low_pass)
low_back.defvjp(back_keep, back_low)

def dense(left_rows, matrix):
    return jnp.dot(left_rows, matrix, precision=precise, preferred_element_type=jnp.float32)

def rms_rows(rows_in, gain_row):
    return rows_in * lax.rsqrt(lax.optimization_barrier(jnp.mean(rows_in * rows_in, axis=-1, keepdims=True)) + 1e-06) * gain_row

def unit_norm(source_rows):
    return source_rows * lax.rsqrt(lax.optimization_barrier(jnp.sum(source_rows * source_rows, axis=-1, keepdims=True)) + 1e-06)

def causal_conv(raw_rows, weight, seq_start):
    positions = jnp.arange(raw_rows.shape[0], dtype=jnp.int32)
    result = raw_rows * weight[0]
    for tap_shift in range(1, weight.shape[0]):
        shifted = jnp.concatenate([jnp.zeros((tap_shift, raw_rows.shape[1]), jnp.float32), raw_rows[:-tap_shift]], axis=0)
        valid_taps = positions - tap_shift >= seq_start
        result = result + jnp.where(valid_taps[:, None], shifted, 0.0) * weight[tap_shift]
    return result

def unit_inverse(lower_part):
    identity = jnp.eye(STRETCH, dtype=jnp.float32)
    inverse = identity - lower_part
    power_term = jnp.einsum('hts,hsu->htu', lower_part, lower_part, precision=precise)
    repeats = STRETCH.bit_length() - 2
    for repeat in range(repeats):
        inverse = inverse + jnp.einsum('hts,hsu->htu', inverse, power_term, precision=precise)
        if repeat + 1 < repeats:
            power_term = jnp.einsum('hts,hsu->htu', power_term, power_term, precision=precise)
    return inverse

def stretch_step(carry_state, inputs):
    query_block, key_block, value_block, beta_block, decay_block, keep_flag = inputs
    carry_state = carry_state * keep_flag
    inclusive = jnp.tri(STRETCH, dtype=bool)
    strict = jnp.tri(STRETCH, k=-1, dtype=bool)
    cumulative = jnp.cumsum(decay_block, axis=-1)
    spread = cumulative[:, :, None] - cumulative[:, None, :]
    within = jnp.where(inclusive, jnp.exp(jnp.where(inclusive, spread, 0.0)), 0.0)
    key_inner = jnp.einsum('htd,hsd->hts', key_block, key_block, precision=precise)
    lower_part = jnp.where(strict, beta_block[:, :, None] * key_inner * within, 0.0)
    inverse = unit_inverse(lower_part)
    growth = jnp.exp(cumulative)
    right_side = jnp.concatenate([(beta_block * growth)[:, :, None] * key_block, beta_block[:, :, None] * value_block], axis=-1)
    solved = jnp.einsum('hts,hsd->htd', inverse, right_side, precision=precise)
    key_part = solved[:, :, :DK]
    value_part = solved[:, :, DK:]
    fresh_rows = value_part - jnp.einsum('htd,hde->hte', key_part, carry_state, precision=precise)
    scores = jnp.einsum('htd,hsd->hts', query_block, key_block, precision=precise) * within
    block_out = growth[:, :, None] * jnp.einsum('htd,hde->hte', query_block, carry_state, precision=precise)
    block_out = block_out + jnp.einsum('hts,hse->hte', scores, fresh_rows, precision=precise)
    last_sum = cumulative[:, -1:]
    tail_decay = jnp.exp(last_sum - cumulative)
    new_state = jnp.exp(last_sum)[:, :, None] * carry_state
    new_state = new_state + jnp.einsum('htd,hte->hde', key_block * tail_decay[:, :, None], fresh_rows, precision=precise)
    return (new_state, block_out)

def delta_rule(queries, key_rows, values, beta_rows, decays, keep_state):
    stretch_count = keep_state.shape[0]
    head_count = queries.shape[1]

    def split_stretches(source):
        shaped = source.reshape((stretch_count, STRETCH) + source.shape[1:])
        return jnp.moveaxis(shaped, 2, 1)
    inputs = (split_stretches(queries), split_stretches(key_rows), split_stretches(values), split_stretches(beta_rows), split_stretches(decays), keep_state)
    first_state = jnp.zeros((head_count, DK, DV), jnp.float32)
    final_state, outputs = lax.scan(jax.checkpoint(stretch_step), first_state, inputs)
    return jnp.moveaxis(outputs, 1, 2).reshape(stretch_count * STRETCH, head_count, DV)

def mixer_core(raw_parts, small_parts, seq_start, keep_state):
    query_raw, key_raw, value_raw, gate_raw, alpha_raw, beta_raw = raw_parts
    query_conv, key_conv, value_conv, log_rate, rate_bias, head_gain = small_parts
    row_count = query_raw.shape[0]
    head_count = alpha_raw.shape[1]
    queries = unit_norm(jax.nn.silu(causal_conv(query_raw, query_conv, seq_start)).reshape(row_count, head_count, DK)) * DK ** (-0.5)
    key_rows = unit_norm(jax.nn.silu(causal_conv(key_raw, key_conv, seq_start)).reshape(row_count, head_count, DK))
    values = jax.nn.silu(causal_conv(value_raw, value_conv, seq_start)).reshape(row_count, head_count, DV)
    beta_rows = jax.nn.sigmoid(beta_raw)
    decays = -jnp.exp(log_rate) * jax.nn.softplus(alpha_raw + rate_bias)
    delta_out = delta_rule(queries, key_rows, values, beta_rows, decays, keep_state)
    normed = delta_out * lax.rsqrt(lax.optimization_barrier(jnp.mean(delta_out * delta_out, axis=-1, keepdims=True)) + 1e-05) * head_gain
    gated_out = normed * jax.nn.silu(gate_raw.reshape(row_count, head_count, DV))
    return gated_out.reshape(row_count, head_count * DV)

def layout(pack_lengths, pack_rows):
    positions = jnp.arange(pack_rows, dtype=jnp.int32)
    first_len = pack_lengths[0].astype(jnp.int32)
    second_len = pack_lengths[1].astype(jnp.int32)
    second_start = (first_len + STRETCH - 1) // STRETCH * STRETCH
    seq_start = jnp.where(positions >= second_start, second_start, 0).astype(jnp.int32)
    live_rows = (positions < first_len) | (positions >= second_start) & (positions < second_start + second_len)
    stretch_starts = jnp.arange(pack_rows // STRETCH, dtype=jnp.int32) * STRETCH
    keep_state = jnp.where((stretch_starts == 0) | (stretch_starts == second_start), 0.0, 1.0).astype(jnp.float32)
    return (seq_start, keep_state, jnp.where(live_rows, 1.0, 0.0).astype(jnp.float32))

def layer_forward(rows_in, weights, seq_start, keep_state, row_mask):
    mixer_gain, query_weight, key_weight, value_weight, outgate_weight, alpha_weight, beta_weight, query_conv, key_conv, value_conv, log_rate, rate_bias, head_gain, output_weight, feed_gain, gate_weight, up_weight, down_weight = weights
    first_rows = low(rms_rows(rows_in, mixer_gain))
    raw_parts = tuple((low_back(dense(first_rows, matrix)) for matrix in (query_weight, key_weight, value_weight, outgate_weight, alpha_weight, beta_weight)))
    gated = low(mixer_core(raw_parts, (query_conv, key_conv, value_conv, log_rate, rate_bias, head_gain), seq_start, keep_state))
    middle = rows_in + low_back(dense(gated, output_weight))
    second_rows = low(rms_rows(middle, feed_gain))
    gate_pre = low_back(dense(second_rows, gate_weight))
    up_pre = low_back(dense(second_rows, up_weight))
    hidden = low(jax.nn.silu(gate_pre) * up_pre)
    return (middle + dense(hidden, down_weight)) * row_mask[:, None]

def reference(tokens, lengths, mixer_gain, query_weight, key_weight, value_weight, outgate_weight, alpha_weight, beta_weight, query_conv, key_conv, value_conv, log_rate, rate_bias, head_gain, output_weight, feed_gain, gate_weight, up_weight, down_weight, cotangent):
    params = tuple((param.astype(jnp.float32) for param in (mixer_gain, query_weight, key_weight, value_weight, outgate_weight, alpha_weight, beta_weight, query_conv, key_conv, value_conv, log_rate, rate_bias, head_gain, output_weight, feed_gain, gate_weight, up_weight, down_weight)))
    pack_count = tokens.shape[0] * N_DP
    token_packs = tokens.reshape(pack_count, PACK, D)
    length_packs = lengths.reshape(pack_count, 2)
    grad_packs = cotangent.reshape(pack_count, PACK, D)

    def per_pack(grad_total, pack_item):
        pack_tokens, pack_lengths, pack_grad = pack_item
        seq_start, keep_state, row_mask = layout(pack_lengths, PACK)

        def forward(rows_in, weights):
            return layer_forward(rows_in, weights, seq_start, keep_state, row_mask)
        result, pull_back = jax.vjp(forward, pack_tokens.astype(jnp.float32), params)
        input_grad, weight_grads = pull_back(pack_grad.astype(jnp.float32))
        grad_total = jax.tree.map(jnp.add, grad_total, weight_grads)
        return (grad_total, (result.astype(jnp.bfloat16), input_grad))
    grad_init = jax.tree.map(jnp.zeros_like, params)
    grad_sums, (outputs, input_grads) = lax.scan(per_pack, grad_init, (token_packs, length_packs, grad_packs))
    g_mixer_gain, g_query, g_key, g_value, g_outgate, g_alpha, g_beta, g_query_conv, g_key_conv, g_value_conv, g_log_rate, g_rate_bias, g_head_gain, g_output, g_feed_gain, g_gate, g_up, g_down = grad_sums
    return (outputs.reshape(tokens.shape), input_grads.reshape(tokens.shape), g_mixer_gain, g_query, g_key, g_value, g_outgate, g_alpha, g_beta, g_query_conv, g_key_conv, g_value_conv, g_log_rate, g_rate_bias, g_head_gain, g_output, g_feed_gain, g_gate, g_up, g_down)
```

```python
import jax
import jax.numpy as jnp
from jax import lax
from jax.sharding import PartitionSpec as P

DK = 128
DV = 256
STRETCH = 64


precise = lax.Precision.HIGHEST


def product(left_rows, matrix):
    return jnp.dot(left_rows, matrix, preferred_element_type=jnp.float32)


def product_nt(left_rows, matrix):
    return lax.dot_general(
        left_rows, matrix, (((1,), (1,)), ((), ())), preferred_element_type=jnp.float32
    )


def product_tn(left_rows, right_rows):
    return lax.dot_general(
        left_rows, right_rows, (((0,), (0,)), ((), ())), preferred_element_type=jnp.float32
    )


def rms_rows(rows_in, gain_row):
    return (
        rows_in * lax.rsqrt(jnp.mean(rows_in * rows_in, axis=-1, keepdims=True) + 1e-06) * gain_row
    )


def unit_norm(source_rows):
    return source_rows * lax.rsqrt(
        jnp.sum(source_rows * source_rows, axis=-1, keepdims=True) + 1e-06
    )


def causal_conv(raw_rows, weight, seq_start):
    positions = jnp.arange(raw_rows.shape[0], dtype=jnp.int32)
    result = raw_rows * weight[0]
    for tap_shift in range(1, weight.shape[0]):
        shifted = jnp.concatenate(
            [jnp.zeros((tap_shift, raw_rows.shape[1]), jnp.float32), raw_rows[:-tap_shift]], axis=0
        )
        valid_taps = positions - tap_shift >= seq_start
        result = result + jnp.where(valid_taps[:, None], shifted, 0.0) * weight[tap_shift]
    return result


def unit_inverse(lower_part):
    identity = jnp.eye(STRETCH, dtype=jnp.float32)
    inverse = identity - lower_part
    power_term = jnp.einsum("hts,hsu->htu", lower_part, lower_part, precision=precise)
    repeats = STRETCH.bit_length() - 2
    for repeat in range(repeats):
        inverse = inverse + jnp.einsum("hts,hsu->htu", inverse, power_term, precision=precise)
        if repeat + 1 < repeats:
            power_term = jnp.einsum("hts,hsu->htu", power_term, power_term, precision=precise)
    return inverse


def stretch_step(carry_state, inputs):
    query_block, key_block, value_block, beta_block, decay_block, keep_flag = inputs
    carry_state = carry_state * keep_flag
    inclusive = jnp.tri(STRETCH, dtype=bool)
    strict = jnp.tri(STRETCH, k=-1, dtype=bool)
    cumulative = jnp.einsum("ts,hs->ht", inclusive.astype(jnp.float32), decay_block, precision=precise)
    spread = cumulative[:, :, None] - cumulative[:, None, :]
    within = jnp.where(inclusive, jnp.exp(jnp.where(inclusive, spread, 0.0)), 0.0)
    key_inner = jnp.einsum("htd,hsd->hts", key_block, key_block, precision=precise)
    lower_part = jnp.where(strict, beta_block[:, :, None] * key_inner * within, 0.0)
    inverse = unit_inverse(lower_part)
    growth = jnp.exp(cumulative)
    right_side = jnp.concatenate(
        [(beta_block * growth)[:, :, None] * key_block, beta_block[:, :, None] * value_block],
        axis=-1,
    )
    solved = jnp.einsum("hts,hsd->htd", inverse, right_side, precision=precise)
    key_part = solved[:, :, :DK]
    value_part = solved[:, :, DK:]
    fresh_rows = value_part - jnp.einsum("htd,hde->hte", key_part, carry_state, precision=precise)
    scores = jnp.einsum("htd,hsd->hts", query_block, key_block, precision=precise) * within
    block_out = growth[:, :, None] * jnp.einsum(
        "htd,hde->hte", query_block, carry_state, precision=precise
    )
    block_out = block_out + jnp.einsum("hts,hse->hte", scores, fresh_rows, precision=precise)
    last_sum = cumulative[:, -1:]
    tail_decay = jnp.exp(last_sum - cumulative)
    new_state = jnp.exp(last_sum)[:, :, None] * carry_state
    new_state = new_state + jnp.einsum(
        "htd,hte->hde", key_block * tail_decay[:, :, None], fresh_rows, precision=precise
    )
    return (new_state, block_out)


def delta_rule(queries, key_rows, values, beta_rows, decays, keep_state):
    stretch_count = keep_state.shape[0]
    head_count = queries.shape[1]

    def split_stretches(source):
        shaped = source.reshape((stretch_count, STRETCH) + source.shape[1:])
        return jnp.moveaxis(shaped, 2, 1)

    inputs = (
        split_stretches(queries),
        split_stretches(key_rows),
        split_stretches(values),
        split_stretches(beta_rows),
        split_stretches(decays),
        keep_state,
    )
    first_state = jnp.zeros((head_count, DK, DV), jnp.float32)
    final_state, outputs = lax.scan(jax.checkpoint(stretch_step), first_state, inputs)
    return jnp.moveaxis(outputs, 1, 2).reshape(stretch_count * STRETCH, head_count, DV)


def mixer_core(raw_parts, small_parts, seq_start, keep_state):
    query_raw, key_raw, value_raw, gate_raw, alpha_raw, beta_raw = raw_parts
    query_conv, key_conv, value_conv, log_rate, rate_bias, head_gain = small_parts
    row_count = query_raw.shape[0]
    head_count = alpha_raw.shape[1]
    queries = unit_norm(
        jax.nn.silu(causal_conv(query_raw, query_conv, seq_start)).reshape(
            row_count, head_count, DK
        )
    ) * DK ** (-0.5)
    key_rows = unit_norm(
        jax.nn.silu(causal_conv(key_raw, key_conv, seq_start)).reshape(row_count, head_count, DK)
    )
    values = jax.nn.silu(causal_conv(value_raw, value_conv, seq_start)).reshape(
        row_count, head_count, DV
    )
    beta_rows = jax.nn.sigmoid(beta_raw)
    decays = -jnp.exp(log_rate) * jax.nn.softplus(alpha_raw + rate_bias)
    delta_out = delta_rule(queries, key_rows, values, beta_rows, decays, keep_state)
    normed = (
        delta_out
        * lax.rsqrt(jnp.mean(delta_out * delta_out, axis=-1, keepdims=True) + 1e-05)
        * head_gain
    )
    gated_out = normed * jax.nn.silu(gate_raw.reshape(row_count, head_count, DV))
    return gated_out.reshape(row_count, head_count * DV)


def layout(pack_lengths, pack_rows):
    positions = jnp.arange(pack_rows, dtype=jnp.int32)
    first_len = pack_lengths[0]
    second_len = pack_lengths[1]
    second_start = (first_len + STRETCH - 1) // STRETCH * STRETCH
    seq_start = jnp.where(positions >= second_start, second_start, 0)
    live_rows = (positions < first_len) | (positions >= second_start) & (
        positions < second_start + second_len
    )
    stretch_starts = jnp.arange(pack_rows // STRETCH, dtype=jnp.int32) * STRETCH
    keep_state = jnp.where(
        (stretch_starts == 0) | (stretch_starts == second_start), 0.0, 1.0
    ).astype(jnp.float32)
    return (seq_start, keep_state, jnp.where(live_rows, 1.0, 0.0).astype(jnp.float32))


LANES = 128


def z_gather(own):
    count = lax.axis_size("tensor")
    if count != 4:
        return lax.all_gather(own, "tensor", axis=0, tiled=True)
    t = lax.axis_index("tensor")
    right = lax.ppermute(own, "tensor", [(0, 1), (1, 2), (2, 3)])
    left = lax.ppermute(own, "tensor", [(1, 0), (2, 1), (3, 2)])
    right2 = lax.ppermute(right, "tensor", [(1, 2), (2, 3)])
    left2 = lax.ppermute(left, "tensor", [(1, 0), (2, 1)])
    far = lax.ppermute(jnp.where(t == 1, right, left), "tensor", [(1, 3), (2, 0)])

    def pick(a, b, c, d):
        return jnp.where(t == 0, a, jnp.where(t == 1, b, jnp.where(t == 2, c, d)))

    return jnp.concatenate(
        [
            pick(own, right, right2, far),
            pick(left, own, right, right2),
            pick(left2, left, own, right),
            pick(far, left2, left, own),
        ],
        axis=0,
    )


def z_scatter(partial):
    count = lax.axis_size("tensor")
    if count != 4:
        return lax.psum_scatter(
            partial.astype(jnp.bfloat16), "tensor", scatter_dimension=0, tiled=True
        ).astype(jnp.float32)
    t = lax.axis_index("tensor")
    rows = partial.shape[0] // count
    parts = partial.reshape(count, rows, partial.shape[1])
    low = parts.astype(jnp.bfloat16)

    def take(source, index):
        return lax.dynamic_index_in_dim(source, jnp.clip(index, 0, count - 1), 0, keepdims=False)

    far = lax.ppermute(jnp.where(t == 3, low[0], low[3]), "tensor", [(3, 1), (0, 2)])
    left = lax.ppermute(take(low, t - 2), "tensor", [(3, 2), (2, 1)])
    right = lax.ppermute(take(low, t + 2), "tensor", [(0, 1), (1, 2)])
    wide = jnp.float32
    to_left = take(parts, t - 1) + left.astype(wide) + jnp.where(t == 1, far, 0).astype(wide)
    to_right = take(parts, t + 1) + right.astype(wide) + jnp.where(t == 2, far, 0).astype(wide)
    from_right = lax.ppermute(to_left.astype(jnp.bfloat16), "tensor", [(1, 0), (2, 1), (3, 2)])
    from_left = lax.ppermute(to_right.astype(jnp.bfloat16), "tensor", [(0, 1), (1, 2), (2, 3)])
    return take(parts, t) + from_right.astype(wide) + from_left.astype(wide)


def sum_over(values, axis):
    count = lax.axis_size(axis)
    if count & (count - 1):
        return lax.psum(values, axis)
    step = 1
    while step < count:
        values = values + lax.ppermute(values, axis, [(i, i ^ step) for i in range(count)])
        step *= 2
    return values


def gather_rows(local):
    return lax.all_gather(local, "dp", axis=0, tiled=True)


def scatter_rows(partial):
    return lax.psum_scatter(
        partial.astype(jnp.bfloat16), "dp", scatter_dimension=0, tiled=True
    ).astype(jnp.float32)


def shards(
    tokens,
    lengths,
    mixer_gain,
    query_weight,
    key_weight,
    value_weight,
    outgate_weight,
    alpha_weight,
    beta_weight,
    query_conv,
    key_conv,
    value_conv,
    log_rate,
    rate_bias,
    head_gain,
    output_weight,
    feed_gain,
    gate_weight,
    up_weight,
    down_weight,
    cotangent,
):
    tensor_index = lax.axis_index("tensor")
    tensor_count = lax.axis_size("tensor")
    micro_count, local_rows, width = tokens.shape
    pack_rows = local_rows * tensor_count
    key_width = query_weight.shape[1]
    value_width = value_weight.shape[1]
    head_count = alpha_weight.shape[1]
    hidden_width = gate_weight.shape[1]
    low = jnp.bfloat16

    edges = (key_width, 2 * key_width, 2 * key_width + value_width, 2 * key_width + 2 * value_width)
    pad = -(2 * head_count) % LANES
    in_local = jnp.concatenate(
        [
            query_weight,
            key_weight,
            value_weight,
            outgate_weight,
            alpha_weight,
            beta_weight,
            jnp.zeros((query_weight.shape[0], pad), low),
        ],
        axis=1,
    )
    in_full = gather_rows(in_local)
    out_full = gather_rows(output_weight.T)
    feed_full = gather_rows(jnp.concatenate([gate_weight, up_weight], axis=1))
    down_full = gather_rows(down_weight.T)

    small_local = (
        lax.dynamic_slice_in_dim(query_conv, tensor_index * key_width, key_width, 1),
        lax.dynamic_slice_in_dim(key_conv, tensor_index * key_width, key_width, 1),
        lax.dynamic_slice_in_dim(value_conv, tensor_index * value_width, value_width, 1),
        lax.dynamic_slice_in_dim(log_rate, tensor_index * head_count, head_count, 0),
        lax.dynamic_slice_in_dim(rate_bias, tensor_index * head_count, head_count, 0),
        head_gain,
    )
    packs = range(micro_count)
    wide = jnp.float32
    token_rows = [tokens[m].astype(wide) for m in packs]
    layouts = [layout(lengths[m, 0], pack_rows) for m in packs]
    own_masks = [
        lax.dynamic_slice_in_dim(row_mask, tensor_index * local_rows, local_rows, 0)[:, None]
        for _, _, row_mask in layouts
    ]
    out_grads = [cotangent[m].astype(wide) * own_masks[m] for m in packs]
    norm_ones = [jax.vjp(rms_rows, token_rows[m], mixer_gain) for m in packs]
    first_rows = [z_gather(norm_ones[m][0].astype(low)) for m in packs]
    grad_rows = [z_gather(out_grads[m].astype(low)) for m in packs]

    cores, gated, middle, norm_twos, second_rows = [], [], [], [], []
    for m in packs:
        raw = product(first_rows[m], in_full)
        raw_parts = (
            raw[:, : edges[0]],
            raw[:, edges[0] : edges[1]],
            raw[:, edges[1] : edges[2]],
            raw[:, edges[2] : edges[3]],
            raw[:, edges[3] : edges[3] + head_count],
            raw[:, edges[3] + head_count : edges[3] + 2 * head_count],
        )
        seq_start, keep_state, _ = layouts[m]

        def core_apply(raw_inputs, small_inputs, seq_start=seq_start, keep_state=keep_state):
            return mixer_core(raw_inputs, small_inputs, seq_start, keep_state)

        mixed, core_back = jax.vjp(core_apply, raw_parts, small_local)
        cores.append(core_back)
        gated.append(mixed.astype(low))
    for m in packs:
        middle.append(token_rows[m] + z_scatter(product_nt(gated[m], out_full)))
        norm_twos.append(jax.vjp(rms_rows, middle[m], feed_gain))
        second_rows.append(z_gather(norm_twos[m][0].astype(low)))

    outputs, hidden, feed_grads, middle_grads, mix_rows = [], [], [], [], []
    small_terms = []
    for m in packs:
        pre = product(second_rows[m], feed_full)
        gate_pre, up_pre = pre[:, :hidden_width], pre[:, hidden_width:]
        gate_sig = jax.nn.sigmoid(gate_pre)
        gate_act = gate_pre * gate_sig
        hidden.append((gate_act * up_pre).astype(low))
        hidden_grad = product(grad_rows[m], down_full)
        gate_grad = hidden_grad * up_pre * gate_sig * (1.0 + gate_pre * (1.0 - gate_sig))
        feed_grads.append(jnp.concatenate([gate_grad, hidden_grad * gate_act], axis=1).astype(low))
        second_grad = z_scatter(product_nt(feed_grads[m], feed_full))
        middle_norm_grad, feed_gain_grad = norm_twos[m][1](second_grad)
        middle_grads.append(out_grads[m] + middle_norm_grad)
        mix_rows.append(z_gather(middle_grads[m].astype(low)))
        result = middle[m] + z_scatter(product_nt(hidden[m], down_full))
        outputs.append((result * own_masks[m]).astype(low))
        small_terms.append([feed_gain_grad])
    joined = lambda parts: jnp.concatenate(parts, axis=0)
    feed_final = scatter_rows(product_tn(joined(second_rows), joined(feed_grads)))
    down_final = scatter_rows(product_tn(joined(grad_rows), joined(hidden)))
    out_final = scatter_rows(product_tn(joined(mix_rows), joined(gated)))

    raw_grads, input_grads = [], []
    for m in packs:
        parts, small_grads = cores[m](product(mix_rows[m], out_full))
        raw_grads.append(
            jnp.concatenate([*parts, jnp.zeros((pack_rows, pad), wide)], axis=1).astype(low)
        )
        first_grad = z_scatter(product_nt(raw_grads[m], in_full))
        token_norm_grad, mixer_gain_grad = norm_ones[m][1](first_grad)
        input_grads.append(middle_grads[m] + token_norm_grad)
        small_terms[m] += [mixer_gain_grad, *small_grads]
    in_final = scatter_rows(product_tn(joined(first_rows), joined(raw_grads)))

    feed_gain_grad, mixer_gain_grad, *core_grads = [sum(terms) for terms in zip(*small_terms)]
    conv_grads = jnp.concatenate(core_grads[:3], axis=1)
    rates = jnp.concatenate(core_grads[3:5])
    everywhere = jnp.concatenate([feed_gain_grad, mixer_gain_grad, core_grads[5]])
    per_slice = jnp.concatenate([conv_grads.reshape(-1), rates])
    packed = sum_over(jnp.concatenate([per_slice, everywhere]), "dp")
    slices = jnp.zeros((tensor_count, per_slice.size), wide)
    slices = lax.dynamic_update_index_in_dim(slices, packed[: per_slice.size], tensor_index, 0)
    packed = sum_over(jnp.concatenate([slices.reshape(-1), packed[per_slice.size :]]), "tensor")
    slices = packed[: slices.size].reshape(tensor_count, per_slice.size)
    taps = query_conv.shape[0]
    conv_all = slices[:, : conv_grads.size].reshape(tensor_count, taps, -1)

    def all_columns(begin, end):
        return jnp.moveaxis(conv_all[:, :, begin:end], 0, 1).reshape(taps, -1)

    rate_all = slices[:, conv_grads.size :]
    everywhere = packed[slices.size :]
    return (
        jnp.stack(outputs),
        jnp.stack(input_grads),
        everywhere[width : 2 * width],
        in_final[:, : edges[0]],
        in_final[:, edges[0] : edges[1]],
        in_final[:, edges[1] : edges[2]],
        in_final[:, edges[2] : edges[3]],
        in_final[:, edges[3] : edges[3] + head_count],
        in_final[:, edges[3] + head_count : edges[3] + 2 * head_count],
        all_columns(0, edges[0]),
        all_columns(edges[0], edges[1]),
        all_columns(edges[1], edges[2]),
        rate_all[:, :head_count].reshape(-1),
        rate_all[:, head_count:].reshape(-1),
        everywhere[2 * width :],
        out_final.T,
        everywhere[:width],
        feed_final[:, :hidden_width],
        feed_final[:, hidden_width:],
        down_final.T,
    )


def solution(mesh):
    return jax.shard_map(
        shards,
        mesh=mesh,
        in_specs=(
            P(None, ("dp", "tensor"), None),
            P(None, "dp", None),
            P(),
            P("dp", "tensor"),
            P("dp", "tensor"),
            P("dp", "tensor"),
            P("dp", "tensor"),
            P("dp", "tensor"),
            P("dp", "tensor"),
            P(),
            P(),
            P(),
            P(),
            P(),
            P(),
            P("tensor", "dp"),
            P(),
            P("dp", "tensor"),
            P("dp", "tensor"),
            P("tensor", "dp"),
            P(None, ("dp", "tensor"), None),
        ),
        out_specs=(
            P(None, ("dp", "tensor"), None),
            P(None, ("dp", "tensor"), None),
            P(),
            P("dp", "tensor"),
            P("dp", "tensor"),
            P("dp", "tensor"),
            P("dp", "tensor"),
            P("dp", "tensor"),
            P("dp", "tensor"),
            P(),
            P(),
            P(),
            P(),
            P(),
            P(),
            P("tensor", "dp"),
            P(),
            P("dp", "tensor"),
            P("dp", "tensor"),
            P("tensor", "dp"),
        ),
        check_vma=False,
    )
```

```python
import functools
import jax
import jax.numpy as jnp
from jax import lax
from jax.experimental import pallas as pl
from jax.experimental.pallas import tpu as pltpu
from jax.sharding import PartitionSpec as P

DK = 128
DV = 256
STRETCH = 64
LANES = 128
HALO = 8
F32 = jnp.float32
LOW = jnp.bfloat16

NN = (((1,), (0,)), ((), ()))
NT = (((1,), (1,)), ((), ()))
TN = (((0,), (0,)), ((), ()))


def split(a):
    hi = a.astype(LOW)
    return hi, (a - hi.astype(F32)).astype(LOW)


def mm(a, b, dims=NN, passes=1):
    if passes == 6:
        return lax.dot_general(a, b, dims, precision=lax.Precision.HIGHEST, preferred_element_type=F32)
    dot = functools.partial(lax.dot_general, dimension_numbers=dims, preferred_element_type=F32)
    if passes == 1:
        return dot(a.astype(LOW), b.astype(LOW))
    ah, al = split(a)
    bh, bl = split(b)
    return dot(ah, bh) + (dot(ah, bl) + dot(al, bh))


def block_masks():
    row = lax.broadcasted_iota(jnp.int32, (STRETCH, STRETCH), 0)
    col = lax.broadcasted_iota(jnp.int32, (STRETCH, STRETCH), 1)
    return row, col


def sigmoid(v):
    return 1.0 / (1.0 + jnp.exp(-v))


def softplus(v):
    return jnp.maximum(v, 0.0) + jnp.log1p(jnp.exp(-jnp.abs(v)))


def unit_inverses(lowers, passes):
    row, col = block_masks()
    eye = jnp.where(row == col, 1.0, 0.0)
    pair = (row // 2 == col // 2) & (row > col)
    inverses = [eye - jnp.where(pair, lower, 0.0) for lower in lowers]
    size = 2
    while size < STRETCH:
        off = (row // (2 * size) == col // (2 * size)) & (row // size > col // size)
        offs = [jnp.where(off, lower, 0.0) for lower in lowers]
        halves = [mm(inv, o, NN, passes) for inv, o in zip(inverses, offs)]
        inverses = [inv - mm(h, inv, NN, passes) for inv, h in zip(inverses, halves)]
        size *= 2
    return inverses


def decay_parts(mixed, rates, heads):
    lane = lax.broadcasted_iota(jnp.int32, (STRETCH, LANES), 1)
    row, col = block_masks()
    soft_in = mixed + rates[1:2, :]
    decay = jnp.where(lane < heads, -jnp.exp(rates[0:1, :]) * softplus(soft_in), 0.0)
    tri = jnp.where(row >= col, 1.0, 0.0)
    upper = jnp.where(row <= col, 1.0, 0.0)
    sum_col = mm(tri, decay, NN, 6)
    sum_row = mm(decay[:, :HALO], upper, TN, 6)
    return decay, soft_in, sum_col, sum_row


def forward_kernel(heads, keep_ref, raw_ref, conv_ref, rates_ref, gain_ref,
                   gated_ref, conved_ref, fresh_ref, out_ref, inv_ref, start_ref, state, ext):
    n = pl.program_id(0)
    keep = keep_ref[n].astype(F32)
    kw, vw = heads * DK, heads * DV
    qkv = 2 * kw + vw
    span = STRETCH

    @pl.when(n == 0)
    def _():
        state[...] = jnp.zeros_like(state)
        ext[...] = jnp.zeros_like(ext)

    ext[0:HALO, :] = ext[span:span + HALO, :] * keep
    ext[HALO:HALO + span, :] = raw_ref[:, :qkv]

    def conv(begin, width):
        total = ext[HALO:HALO + span, begin:begin + width] * conv_ref[0:1, begin:begin + width]
        for j in range(1, 4):
            total = total + ext[HALO - j:HALO - j + span, begin:begin + width] * conv_ref[j:j + 1, begin:begin + width]
        conved_ref[:, begin:begin + width] = total
        return total * sigmoid(total)

    mixed = raw_ref[:, qkv + vw:]
    decay, _, sum_col, sum_row = decay_parts(mixed, rates_ref[...], heads)
    beta_all = sigmoid(mixed)
    row, col = block_masks()
    incl, strict = row >= col, row > col
    qs, ks, lowers, scores, betas = [], [], [], [], []
    for h in range(heads):
        zq = conv(h * DK, DK)
        zk = conv(kw + h * DK, DK)
        q = zq * lax.rsqrt(jnp.sum(zq * zq, axis=-1, keepdims=True) + 1e-6) * DK ** -0.5
        k = zk * lax.rsqrt(jnp.sum(zk * zk, axis=-1, keepdims=True) + 1e-6)
        within = jnp.exp(jnp.where(incl, sum_col[:, h:h + 1] - sum_row[h:h + 1, :], -1e30))
        beta = beta_all[:, heads + h:heads + h + 1]
        scores.append(mm(q, k, NT, 3) * within)
        lowers.append(jnp.where(strict, beta * mm(k, k, NT, 3) * within, 0.0))
        qs.append(q); ks.append(k); betas.append(beta)
    inverses = unit_inverses(lowers, 3)
    for h in range(heads):
        q, k, beta = qs[h], ks[h], betas[h]
        start = state[h] * keep
        total = sum_col[:, h:h + 1]
        growth = jnp.exp(total)
        last = total[span - 1:span, :]
        v = conv(2 * kw + h * DV, DV)
        k_state = mm(k, start, NN, 3)
        q_state = mm(q, start, NN, 3)
        fresh = mm(inverses[h], beta * (v - growth * k_state), NN, 3)
        out = growth * q_state + mm(scores[h], fresh, NN, 3)
        tail = jnp.exp(last - total)
        state[h] = jnp.exp(last) * start + mm(k * tail, fresh, TN, 3)
        cols = slice(h * DV, (h + 1) * DV)
        fresh_ref[:, cols] = fresh.astype(fresh_ref.dtype)
        out_ref[:, cols] = out
        inv_ref[0, h] = inverses[h].astype(inv_ref.dtype)
        start_ref[0, h] = start.astype(start_ref.dtype)
        gate = raw_ref[:, qkv + h * DV:qkv + (h + 1) * DV]
        normed = out * lax.rsqrt(jnp.mean(out * out, axis=-1, keepdims=True) + 1e-5) * gain_ref[...]
        gated_ref[:, cols] = (normed * (gate * sigmoid(gate))).astype(LOW)


def mixer_forward(raw, keep, conv, rates, gain, heads):
    rows, width = raw.shape
    count = rows // STRETCH
    kw, vw = heads * DK, heads * DV
    qkv = 2 * kw + vw
    at = lambda n, keep_ref: (n, 0)
    fixed = lambda n, keep_ref: (0, 0)
    at4 = lambda n, keep_ref: (n, 0, 0, 0)
    spec = pl.BlockSpec
    return pl.pallas_call(
        functools.partial(forward_kernel, heads),
        grid_spec=pltpu.PrefetchScalarGridSpec(
            num_scalar_prefetch=1,
            grid=(count,),
            in_specs=[spec((STRETCH, width), at), spec((4, qkv), fixed), spec((HALO, LANES), fixed), spec((1, DV), fixed)],
            out_specs=[
                spec((STRETCH, vw), at),
                spec((STRETCH, qkv), at),
                spec((STRETCH, vw), at),
                spec((STRETCH, vw), at),
                spec((1, heads, STRETCH, STRETCH), at4),
                spec((1, heads, DK, DV), at4),
            ],
            scratch_shapes=[pltpu.VMEM((heads, DK, DV), F32), pltpu.VMEM((STRETCH + HALO, qkv), F32)],
        ),
        out_shape=[
            jax.ShapeDtypeStruct((rows, vw), LOW),
            jax.ShapeDtypeStruct((rows, qkv), F32),
            jax.ShapeDtypeStruct((rows, vw), F32),
            jax.ShapeDtypeStruct((rows, vw), F32),
            jax.ShapeDtypeStruct((count, heads, STRETCH, STRETCH), F32),
            jax.ShapeDtypeStruct((count, heads, DK, DV), F32),
        ],
        compiler_params=pltpu.CompilerParams(dimension_semantics=("arbitrary",), vmem_limit_bytes=32 << 20),
        cost_estimate=pl.CostEstimate(flops=3 * 10**10, bytes_accessed=30 << 20, transcendentals=0),
        name="mixer_forward",
    )(keep, raw, conv, rates, gain)


def backward_kernel(heads, keep_ref, raw_ref, conved_ref, fresh_ref, out_ref, inv_ref, start_ref, grad_ref,
                    conv_ref, rates_ref, gain_ref,
                    draw_ref, dconv_ref, drates_ref, dgain_ref, dstate, ext):
    i = pl.program_id(0)
    count = pl.num_programs(0)
    n = count - 1 - i
    keep_next = keep_ref[n + 1].astype(F32)
    kw, vw = heads * DK, heads * DV
    qkv = 2 * kw + vw
    span = STRETCH

    @pl.when(i == 0)
    def _():
        dstate[...] = jnp.zeros_like(dstate)
        ext[...] = jnp.zeros_like(ext)
        dconv_ref[...] = jnp.zeros_like(dconv_ref)
        drates_ref[...] = jnp.zeros_like(drates_ref)
        dgain_ref[...] = jnp.zeros_like(dgain_ref)

    ext[span:span + HALO, :] = ext[0:HALO, :] * keep_next
    rates = rates_ref[...]
    mixed = raw_ref[:, qkv + vw:]
    decay, soft_in, sum_col, sum_row = decay_parts(mixed, rates, heads)
    beta_all = sigmoid(mixed)
    row, col = block_masks()
    incl, strict = row >= col, row > col
    lane = lax.broadcasted_iota(jnp.int32, (span, LANES), 1)
    last_row = lax.broadcasted_iota(jnp.int32, (span, 1), 0) == span - 1
    gain = gain_ref[...]
    dgain = jnp.zeros((1, DV), F32)
    dsum_all = jnp.zeros((span, LANES), F32)
    dbeta_all = jnp.zeros((span, LANES), F32)
    down_rows = []

    def act(begin, width):
        c = conved_ref[:, begin:begin + width]
        s = sigmoid(c)
        return c * s, s * (1.0 + c * (1.0 - s))

    for h in range(heads):
        cols = slice(h * DV, (h + 1) * DV)
        zq, slope_q = act(h * DK, DK)
        zk, slope_k = act(kw + h * DK, DK)
        v, slope_v = act(2 * kw + h * DV, DV)
        rq = lax.rsqrt(jnp.sum(zq * zq, axis=-1, keepdims=True) + 1e-6)
        rk = lax.rsqrt(jnp.sum(zk * zk, axis=-1, keepdims=True) + 1e-6)
        q = zq * rq * DK ** -0.5
        k = zk * rk
        within = jnp.exp(jnp.where(incl, sum_col[:, h:h + 1] - sum_row[h:h + 1, :], -1e30))
        beta = beta_all[:, heads + h:heads + h + 1]
        total = sum_col[:, h:h + 1]
        growth = jnp.exp(total)
        last = total[span - 1:span, :]
        growth_last = jnp.exp(last)
        tail = jnp.exp(last - total)
        start = start_ref[0, h].astype(F32)
        fresh = fresh_ref[:, cols].astype(F32)
        inv = inv_ref[0, h]
        scores = mm(q, k, NT, 3) * within
        inner = mm(k, k, NT, 3)
        k_state = mm(k, start, NN, 3)
        q_state = mm(q, start, NN, 3)
        out = out_ref[:, cols]
        gate = raw_ref[:, qkv + h * DV:qkv + (h + 1) * DV]
        gate_sig = sigmoid(gate)
        gate_act = gate * gate_sig
        dgated = grad_ref[:, cols].astype(F32)
        r = lax.rsqrt(jnp.mean(out * out, axis=-1, keepdims=True) + 1e-5)
        unit = out * r
        dnormed = dgated * gate_act
        draw_ref[:, qkv + h * DV:qkv + (h + 1) * DV] = (
            dgated * (unit * gain) * (gate_sig * (1.0 + gate * (1.0 - gate_sig)))
        ).astype(LOW)
        dgain = dgain + jnp.sum(dnormed * unit, axis=0, keepdims=True)
        dunit = dnormed * gain
        dout = r * (dunit - unit * jnp.mean(dunit * unit, axis=-1, keepdims=True))
        dnext = dstate[h] * keep_next
        dfresh = mm(scores, dout, TN, 3) + mm(k * tail, dnext, NN, 3)
        dright = mm(inv, dfresh, TN, 3)
        dscores = jnp.where(incl, mm(dout, fresh, NT, 3), 0.0)
        dlower = jnp.where(strict, -mm(dright, fresh, NT, 3), 0.0)
        scaled = beta * growth * dright
        dstate[h] = growth_last * dnext + mm(q * growth, dout, TN, 3) - mm(k, scaled, TN, 3)
        dv = beta * dright
        dbeta = jnp.sum(dright * (v - growth * k_state), axis=-1, keepdims=True)
        dgrowth = jnp.sum(dout * q_state - dv * k_state, axis=-1, keepdims=True)
        dsw = dscores * within
        dq = growth * mm(dout, start, NT, 3) + mm(dsw, k, NN, 3)
        into_k = mm(fresh, dnext, NT, 3)
        dinner = dlower * within
        dbeta = dbeta + jnp.sum(dinner * inner, axis=-1, keepdims=True)
        weighted = beta * dinner
        dk = (
            tail * into_k
            - mm(scaled, start, NT, 3)
            + mm(dsw, q, TN, 3)
            + mm(weighted, k, NN, 3)
            + mm(weighted, k, TN, 3)
        )
        tailed = tail * jnp.sum(k * into_k, axis=-1, keepdims=True)
        pairs = dscores * scores + weighted * inner
        at_last = growth_last * jnp.sum(start * dnext, keepdims=True) + jnp.sum(tailed, keepdims=True)
        dsum = jnp.sum(pairs, axis=-1, keepdims=True) + growth * dgrowth - tailed + jnp.where(last_row, at_last, 0.0)
        down_rows.append(jnp.sum(pairs, axis=0, keepdims=True))
        dsum_all = jnp.where(lane == h, dsum, dsum_all)
        dbeta_all = jnp.where(lane == heads + h, dbeta, dbeta_all)
        dzq = (DK ** -0.5 * rq) * (dq - zq * (rq * rq * jnp.sum(dq * zq, axis=-1, keepdims=True)))
        dzk = rk * (dk - zk * (rk * rk * jnp.sum(dk * zk, axis=-1, keepdims=True)))
        ext[0:span, h * DK:(h + 1) * DK] = dzq * slope_q
        ext[0:span, kw + h * DK:kw + (h + 1) * DK] = dzk * slope_k
        ext[0:span, 2 * kw + h * DV:2 * kw + (h + 1) * DV] = dv * slope_v

    dgain_ref[...] += dgain
    upper = jnp.where(row <= col, 1.0, 0.0)
    down = jnp.concatenate(down_rows + [jnp.zeros((LANES - heads, span), F32)], axis=0)
    ddecay = mm(upper, dsum_all, NN, 6) - mm(upper, down, NT, 6)
    ddecay = jnp.where(lane < heads, ddecay, 0.0)
    dalpha = ddecay * (-jnp.exp(rates[0:1, :])) * sigmoid(soft_in)
    dbeta_raw = jnp.where((lane >= heads) & (lane < 2 * heads), dbeta_all * beta_all * (1.0 - beta_all), 0.0)
    draw_ref[:, qkv + vw:] = (dalpha + dbeta_raw).astype(LOW)
    drates_ref[0:1, :] += jnp.sum(ddecay * decay, axis=0, keepdims=True)
    drates_ref[1:2, :] += jnp.sum(dalpha, axis=0, keepdims=True)
    wide = 256
    for begin in range(0, qkv, wide):
        cols = slice(begin, begin + wide)
        raw = raw_ref[:, cols]
        total = None
        for j in range(4):
            shifted = ext[j:j + span, cols]
            term = shifted * conv_ref[j:j + 1, cols]
            total = term if total is None else total + term
            dconv_ref[j:j + 1, cols] += jnp.sum(raw * shifted, axis=0, keepdims=True)
        draw_ref[:, cols] = total.astype(LOW)


def mixer_backward(raw, kept, grad, keep, conv, rates, gain, heads):
    conved, fresh, out, inv, start = kept
    rows, width = raw.shape
    count = rows // STRETCH
    kw, vw = heads * DK, heads * DV
    qkv = 2 * kw + vw
    at = lambda i, keep_ref: (count - 1 - i, 0)
    fixed = lambda i, keep_ref: (0, 0)
    at4 = lambda i, keep_ref: (count - 1 - i, 0, 0, 0)
    spec = pl.BlockSpec
    return pl.pallas_call(
        functools.partial(backward_kernel, heads),
        grid_spec=pltpu.PrefetchScalarGridSpec(
            num_scalar_prefetch=1,
            grid=(count,),
            in_specs=[
                spec((STRETCH, width), at),
                spec((STRETCH, qkv), at),
                spec((STRETCH, vw), at),
                spec((STRETCH, vw), at),
                spec((1, heads, STRETCH, STRETCH), at4),
                spec((1, heads, DK, DV), at4),
                spec((STRETCH, vw), at),
                spec((4, qkv), fixed),
                spec((HALO, LANES), fixed),
                spec((1, DV), fixed),
            ],
            out_specs=[spec((STRETCH, width), at), spec((4, qkv), fixed), spec((HALO, LANES), fixed), spec((1, DV), fixed)],
            scratch_shapes=[pltpu.VMEM((heads, DK, DV), F32), pltpu.VMEM((STRETCH + HALO, qkv), F32)],
        ),
        out_shape=[
            jax.ShapeDtypeStruct((rows, width), LOW),
            jax.ShapeDtypeStruct((4, qkv), F32),
            jax.ShapeDtypeStruct((HALO, LANES), F32),
            jax.ShapeDtypeStruct((1, DV), F32),
        ],
        compiler_params=pltpu.CompilerParams(dimension_semantics=("arbitrary",), vmem_limit_bytes=32 << 20),
        cost_estimate=pl.CostEstimate(flops=6 * 10**10, bytes_accessed=40 << 20, transcendentals=0),
        name="mixer_backward",
    )(jnp.concatenate([keep, jnp.zeros((1,), jnp.int32)]), raw, conved, fresh, out, inv, start, grad, conv, rates, gain)


def product(left_rows, matrix):
    return lax.dot_general(left_rows, matrix, NN, preferred_element_type=F32)


def product_nt(left_rows, matrix):
    return lax.dot_general(left_rows, matrix, NT, preferred_element_type=F32)


def product_tn(left_rows, right_rows):
    return lax.dot_general(left_rows, right_rows, TN, preferred_element_type=F32)


def rms_rows(rows_in, gain_row):
    return (
        rows_in * lax.rsqrt(jnp.mean(rows_in * rows_in, axis=-1, keepdims=True) + 1e-06) * gain_row
    )


def layout(pack_lengths, pack_rows):
    positions = jnp.arange(pack_rows, dtype=jnp.int32)
    first_len = pack_lengths[0]
    second_len = pack_lengths[1]
    second_start = (first_len + STRETCH - 1) // STRETCH * STRETCH
    live_rows = (positions < first_len) | (positions >= second_start) & (
        positions < second_start + second_len
    )
    stretch_starts = jnp.arange(pack_rows // STRETCH, dtype=jnp.int32) * STRETCH
    keep_state = jnp.where(
        (stretch_starts == 0) | (stretch_starts == second_start), 0, 1
    ).astype(jnp.int32)
    return (keep_state, jnp.where(live_rows, 1.0, 0.0).astype(jnp.float32))


def z_gather(own):
    count = lax.axis_size("tensor")
    if count != 4:
        return lax.all_gather(own, "tensor", axis=0, tiled=True)
    t = lax.axis_index("tensor")
    right = lax.ppermute(own, "tensor", [(0, 1), (1, 2), (2, 3)])
    left = lax.ppermute(own, "tensor", [(1, 0), (2, 1), (3, 2)])
    right2 = lax.ppermute(right, "tensor", [(1, 2), (2, 3)])
    left2 = lax.ppermute(left, "tensor", [(1, 0), (2, 1)])
    far = lax.ppermute(jnp.where(t == 1, right, left), "tensor", [(1, 3), (2, 0)])

    def pick(a, b, c, d):
        return jnp.where(t == 0, a, jnp.where(t == 1, b, jnp.where(t == 2, c, d)))

    return jnp.concatenate(
        [
            pick(own, right, right2, far),
            pick(left, own, right, right2),
            pick(left2, left, own, right),
            pick(far, left2, left, own),
        ],
        axis=0,
    )


def z_scatter(partial):
    count = lax.axis_size("tensor")
    if count != 4:
        return lax.psum_scatter(
            partial.astype(jnp.bfloat16), "tensor", scatter_dimension=0, tiled=True
        ).astype(jnp.float32)
    t = lax.axis_index("tensor")
    rows = partial.shape[0] // count
    parts = partial.reshape(count, rows, partial.shape[1])
    low = parts.astype(jnp.bfloat16)

    def take(source, index):
        return lax.dynamic_index_in_dim(source, jnp.clip(index, 0, count - 1), 0, keepdims=False)

    far = lax.ppermute(jnp.where(t == 3, low[0], low[3]), "tensor", [(3, 1), (0, 2)])
    left = lax.ppermute(take(low, t - 2), "tensor", [(3, 2), (2, 1)])
    right = lax.ppermute(take(low, t + 2), "tensor", [(0, 1), (1, 2)])
    wide = jnp.float32
    to_left = take(parts, t - 1) + left.astype(wide) + jnp.where(t == 1, far, 0).astype(wide)
    to_right = take(parts, t + 1) + right.astype(wide) + jnp.where(t == 2, far, 0).astype(wide)
    from_right = lax.ppermute(to_left.astype(jnp.bfloat16), "tensor", [(1, 0), (2, 1), (3, 2)])
    from_left = lax.ppermute(to_right.astype(jnp.bfloat16), "tensor", [(0, 1), (1, 2), (2, 3)])
    return take(parts, t) + from_right.astype(wide) + from_left.astype(wide)


def sum_over(values, axis):
    count = lax.axis_size(axis)
    if count & (count - 1):
        return lax.psum(values, axis)
    step = 1
    while step < count:
        values = values + lax.ppermute(values, axis, [(i, i ^ step) for i in range(count)])
        step *= 2
    return values


def gather_rows(local):
    return lax.all_gather(local, "dp", axis=0, tiled=True)


def scatter_rows(partial):
    return lax.psum_scatter(
        partial.astype(jnp.bfloat16), "dp", scatter_dimension=0, tiled=True
    ).astype(jnp.float32)


def shards(
    tokens,
    lengths,
    mixer_gain,
    query_weight,
    key_weight,
    value_weight,
    outgate_weight,
    alpha_weight,
    beta_weight,
    query_conv,
    key_conv,
    value_conv,
    log_rate,
    rate_bias,
    head_gain,
    output_weight,
    feed_gain,
    gate_weight,
    up_weight,
    down_weight,
    cotangent,
):
    tensor_index = lax.axis_index("tensor")
    tensor_count = lax.axis_size("tensor")
    micro_count, local_rows, width = tokens.shape
    pack_rows = local_rows * tensor_count
    key_width = query_weight.shape[1]
    value_width = value_weight.shape[1]
    head_count = alpha_weight.shape[1]
    hidden_width = gate_weight.shape[1]
    low = jnp.bfloat16

    edges = (key_width, 2 * key_width, 2 * key_width + value_width, 2 * key_width + 2 * value_width)
    pad = -(2 * head_count) % LANES
    in_local = jnp.concatenate(
        [
            query_weight,
            key_weight,
            value_weight,
            outgate_weight,
            alpha_weight,
            beta_weight,
            jnp.zeros((query_weight.shape[0], pad), low),
        ],
        axis=1,
    )
    in_full = gather_rows(in_local)
    out_full = gather_rows(output_weight.T)
    feed_full = gather_rows(jnp.concatenate([gate_weight, up_weight], axis=1))
    down_full = gather_rows(down_weight.T)

    small_local = (
        lax.dynamic_slice_in_dim(query_conv, tensor_index * key_width, key_width, 1),
        lax.dynamic_slice_in_dim(key_conv, tensor_index * key_width, key_width, 1),
        lax.dynamic_slice_in_dim(value_conv, tensor_index * value_width, value_width, 1),
        lax.dynamic_slice_in_dim(log_rate, tensor_index * head_count, head_count, 0),
        lax.dynamic_slice_in_dim(rate_bias, tensor_index * head_count, head_count, 0),
        head_gain,
    )
    packs = range(micro_count)
    wide = jnp.float32
    token_rows = [tokens[m].astype(wide) for m in packs]
    layouts = [layout(lengths[m, 0], pack_rows) for m in packs]
    own_masks = [
        lax.dynamic_slice_in_dim(row_mask, tensor_index * local_rows, local_rows, 0)[:, None]
        for _, row_mask in layouts
    ]
    out_grads = [cotangent[m].astype(wide) * own_masks[m] for m in packs]
    norm_ones = [jax.vjp(rms_rows, token_rows[m], mixer_gain) for m in packs]
    first_rows = [z_gather(norm_ones[m][0].astype(low)) for m in packs]
    grad_rows = [z_gather(out_grads[m].astype(low)) for m in packs]

    conv_local = jnp.concatenate(small_local[:3], axis=1)
    rates = jnp.zeros((HALO, LANES), wide)
    rates = rates.at[0, :head_count].set(small_local[3]).at[1, :head_count].set(small_local[4])
    gain_row = head_gain[None, :]
    raws, kept, gated, middle, norm_twos, second_rows = [], [], [], [], [], []
    for m in packs:
        raws.append(product(first_rows[m], in_full))
        mixed, *rest = mixer_forward(
            raws[m], layouts[m][0], conv_local, rates, gain_row, head_count
        )
        kept.append(rest)
        gated.append(mixed)
    for m in packs:
        middle.append(token_rows[m] + z_scatter(product_nt(gated[m], out_full)))
        norm_twos.append(jax.vjp(rms_rows, middle[m], feed_gain))
        second_rows.append(z_gather(norm_twos[m][0].astype(low)))

    outputs, hidden, feed_grads, middle_grads, mix_rows = [], [], [], [], []
    small_terms = []
    for m in packs:
        pre = product(second_rows[m], feed_full)
        gate_pre, up_pre = pre[:, :hidden_width], pre[:, hidden_width:]
        gate_sig = jax.nn.sigmoid(gate_pre)
        gate_act = gate_pre * gate_sig
        hidden.append((gate_act * up_pre).astype(low))
        hidden_grad = product(grad_rows[m], down_full)
        gate_grad = hidden_grad * up_pre * gate_sig * (1.0 + gate_pre * (1.0 - gate_sig))
        feed_grads.append(jnp.concatenate([gate_grad, hidden_grad * gate_act], axis=1).astype(low))
        second_grad = z_scatter(product_nt(feed_grads[m], feed_full))
        middle_norm_grad, feed_gain_grad = norm_twos[m][1](second_grad)
        middle_grads.append(out_grads[m] + middle_norm_grad)
        mix_rows.append(z_gather(middle_grads[m].astype(low)))
        result = middle[m] + z_scatter(product_nt(hidden[m], down_full))
        outputs.append((result * own_masks[m]).astype(low))
        small_terms.append([feed_gain_grad])
    joined = lambda parts: jnp.concatenate(parts, axis=0)
    feed_final = scatter_rows(product_tn(joined(second_rows), joined(feed_grads)))
    down_final = scatter_rows(product_tn(joined(grad_rows), joined(hidden)))
    out_final = scatter_rows(product_tn(joined(mix_rows), joined(gated)))

    raw_grads, input_grads = [], []
    for m in packs:
        raw_grad, conv_grad, rate_grad, gain_grad = mixer_backward(
            raws[m],
            kept[m],
            product(mix_rows[m], out_full),
            layouts[m][0],
            conv_local,
            rates,
            gain_row,
            head_count,
        )
        raw_grads.append(raw_grad)
        first_grad = z_scatter(product_nt(raw_grads[m], in_full))
        token_norm_grad, mixer_gain_grad = norm_ones[m][1](first_grad)
        input_grads.append(middle_grads[m] + token_norm_grad)
        small_terms[m] += [mixer_gain_grad, conv_grad, rate_grad[:2, :head_count], gain_grad[0]]
    in_final = scatter_rows(product_tn(joined(first_rows), joined(raw_grads)))

    feed_gain_grad, mixer_gain_grad, *core_grads = [sum(terms) for terms in zip(*small_terms)]
    conv_grads, rate_grads, gain_grads = core_grads
    everywhere = jnp.concatenate([feed_gain_grad, mixer_gain_grad, gain_grads])
    per_slice = jnp.concatenate([conv_grads.reshape(-1), rate_grads.reshape(-1)])
    packed = sum_over(jnp.concatenate([per_slice, everywhere]), "dp")
    slices = jnp.zeros((tensor_count, per_slice.size), wide)
    slices = lax.dynamic_update_index_in_dim(slices, packed[: per_slice.size], tensor_index, 0)
    packed = sum_over(jnp.concatenate([slices.reshape(-1), packed[per_slice.size :]]), "tensor")
    slices = packed[: slices.size].reshape(tensor_count, per_slice.size)
    taps = query_conv.shape[0]
    conv_all = slices[:, : conv_grads.size].reshape(tensor_count, taps, -1)

    def all_columns(begin, end):
        return jnp.moveaxis(conv_all[:, :, begin:end], 0, 1).reshape(taps, -1)

    rate_all = slices[:, conv_grads.size :]
    everywhere = packed[slices.size :]
    return (
        jnp.stack(outputs),
        jnp.stack(input_grads),
        everywhere[width : 2 * width],
        in_final[:, : edges[0]],
        in_final[:, edges[0] : edges[1]],
        in_final[:, edges[1] : edges[2]],
        in_final[:, edges[2] : edges[3]],
        in_final[:, edges[3] : edges[3] + head_count],
        in_final[:, edges[3] + head_count : edges[3] + 2 * head_count],
        all_columns(0, edges[0]),
        all_columns(edges[0], edges[1]),
        all_columns(edges[1], edges[2]),
        rate_all[:, :head_count].reshape(-1),
        rate_all[:, head_count:].reshape(-1),
        everywhere[2 * width :],
        out_final.T,
        everywhere[:width],
        feed_final[:, :hidden_width],
        feed_final[:, hidden_width:],
        down_final.T,
    )


def solution(mesh):
    return jax.shard_map(
        shards,
        mesh=mesh,
        in_specs=(
            P(None, ("dp", "tensor"), None),
            P(None, "dp", None),
            P(),
            P("dp", "tensor"),
            P("dp", "tensor"),
            P("dp", "tensor"),
            P("dp", "tensor"),
            P("dp", "tensor"),
            P("dp", "tensor"),
            P(),
            P(),
            P(),
            P(),
            P(),
            P(),
            P("tensor", "dp"),
            P(),
            P("dp", "tensor"),
            P("dp", "tensor"),
            P("tensor", "dp"),
            P(None, ("dp", "tensor"), None),
        ),
        out_specs=(
            P(None, ("dp", "tensor"), None),
            P(None, ("dp", "tensor"), None),
            P(),
            P("dp", "tensor"),
            P("dp", "tensor"),
            P("dp", "tensor"),
            P("dp", "tensor"),
            P("dp", "tensor"),
            P("dp", "tensor"),
            P(),
            P(),
            P(),
            P(),
            P(),
            P(),
            P("tensor", "dp"),
            P(),
            P("dp", "tensor"),
            P("dp", "tensor"),
            P("tensor", "dp"),
        ),
        check_vma=False,
    )
```

```python
import functools
import jax
import jax.numpy as jnp
from jax import lax
from jax.experimental import pallas as pl
from jax.experimental.pallas import tpu as pltpu
from jax.sharding import PartitionSpec as P

DK = 128
DV = 256
STRETCH = 64
LANES = 128
HALO = 8
F32 = jnp.float32
LOW = jnp.bfloat16

NN = (((1,), (0,)), ((), ()))
NT = (((1,), (1,)), ((), ()))
TN = (((0,), (0,)), ((), ()))


def split(a):
    hi = a.astype(LOW)
    return hi, (a - hi.astype(F32)).astype(LOW)


def mm(a, b, dims=NN, passes=1):
    if passes == 6:
        return lax.dot_general(a, b, dims, precision=lax.Precision.HIGHEST, preferred_element_type=F32)
    dot = functools.partial(lax.dot_general, dimension_numbers=dims, preferred_element_type=F32)
    if passes == 1:
        return dot(a.astype(LOW), b.astype(LOW))
    ah, al = split(a)
    bh, bl = split(b)
    return dot(ah, bh) + (dot(ah, bl) + dot(al, bh))


def block_masks():
    row = lax.broadcasted_iota(jnp.int32, (STRETCH, STRETCH), 0)
    col = lax.broadcasted_iota(jnp.int32, (STRETCH, STRETCH), 1)
    return row, col


def sigmoid(v):
    return 1.0 / (1.0 + jnp.exp(-v))


def softplus(v):
    return jnp.maximum(v, 0.0) + jnp.log1p(jnp.exp(-jnp.abs(v)))


def unit_inverses(lowers, passes):
    row, col = block_masks()
    eye = jnp.where(row == col, 1.0, 0.0)
    pair = (row // 2 == col // 2) & (row > col)
    inverses = [eye - jnp.where(pair, lower, 0.0) for lower in lowers]
    size = 2
    while size < STRETCH:
        off = (row // (2 * size) == col // (2 * size)) & (row // size > col // size)
        offs = [jnp.where(off, lower, 0.0) for lower in lowers]
        halves = [mm(inv, o, NN, passes) for inv, o in zip(inverses, offs)]
        inverses = [inv - mm(h, inv, NN, passes) for inv, h in zip(inverses, halves)]
        size *= 2
    return inverses


def decay_parts(mixed, rates, heads):
    lane = lax.broadcasted_iota(jnp.int32, (STRETCH, LANES), 1)
    row, col = block_masks()
    soft_in = mixed + rates[1:2, :]
    decay = jnp.where(lane < heads, -jnp.exp(rates[0:1, :]) * softplus(soft_in), 0.0)
    tri = jnp.where(row >= col, 1.0, 0.0)
    upper = jnp.where(row <= col, 1.0, 0.0)
    sum_col = mm(tri, decay, NN, 6)
    sum_row = mm(decay[:, :HALO], upper, TN, 6)
    return decay, soft_in, sum_col, sum_row


def forward_kernel(heads, keep_ref, raw_ref, conv_ref, rates_ref, gain_ref,
                   gated_ref, conved_ref, fresh_ref, out_ref, inv_ref, start_ref, state, ext):
    n = pl.program_id(0)
    keep = keep_ref[n].astype(F32)
    kw, vw = heads * DK, heads * DV
    qkv = 2 * kw + vw
    span = STRETCH

    @pl.when(n == 0)
    def _():
        state[...] = jnp.zeros_like(state)
        ext[...] = jnp.zeros_like(ext)

    ext[0:HALO, :] = ext[span:span + HALO, :] * keep
    ext[HALO:HALO + span, :] = raw_ref[:, :qkv]

    def conv(begin, width):
        total = ext[HALO:HALO + span, begin:begin + width] * conv_ref[0:1, begin:begin + width]
        for j in range(1, 4):
            total = total + ext[HALO - j:HALO - j + span, begin:begin + width] * conv_ref[j:j + 1, begin:begin + width]
        conved_ref[:, begin:begin + width] = total
        return total * sigmoid(total)

    mixed = raw_ref[:, qkv + vw:]
    decay, _, sum_col, sum_row = decay_parts(mixed, rates_ref[...], heads)
    beta_all = sigmoid(mixed)
    row, col = block_masks()
    incl, strict = row >= col, row > col
    qs, ks, lowers, scores, betas = [], [], [], [], []
    for h in range(heads):
        zq = conv(h * DK, DK)
        zk = conv(kw + h * DK, DK)
        q = zq * lax.rsqrt(jnp.sum(zq * zq, axis=-1, keepdims=True) + 1e-6) * DK ** -0.5
        k = zk * lax.rsqrt(jnp.sum(zk * zk, axis=-1, keepdims=True) + 1e-6)
        within = jnp.exp(jnp.where(incl, sum_col[:, h:h + 1] - sum_row[h:h + 1, :], -1e30))
        beta = beta_all[:, heads + h:heads + h + 1]
        scores.append(mm(q, k, NT, 3) * within)
        lowers.append(jnp.where(strict, beta * mm(k, k, NT, 3) * within, 0.0))
        qs.append(q); ks.append(k); betas.append(beta)
    inverses = unit_inverses(lowers, 3)
    for h in range(heads):
        q, k, beta = qs[h], ks[h], betas[h]
        start = state[h] * keep
        total = sum_col[:, h:h + 1]
        growth = jnp.exp(total)
        last = total[span - 1:span, :]
        v = conv(2 * kw + h * DV, DV)
        k_state = mm(k, start, NN, 3)
        q_state = mm(q, start, NN, 3)
        fresh = mm(inverses[h], beta * (v - growth * k_state), NN, 3)
        out = growth * q_state + mm(scores[h], fresh, NN, 3)
        tail = jnp.exp(last - total)
        state[h] = jnp.exp(last) * start + mm(k * tail, fresh, TN, 3)
        cols = slice(h * DV, (h + 1) * DV)
        fresh_ref[:, cols] = fresh.astype(fresh_ref.dtype)
        out_ref[:, cols] = out
        inv_ref[0, h] = inverses[h].astype(inv_ref.dtype)
        start_ref[0, h] = start.astype(start_ref.dtype)
        gate = raw_ref[:, qkv + h * DV:qkv + (h + 1) * DV]
        normed = out * lax.rsqrt(jnp.mean(out * out, axis=-1, keepdims=True) + 1e-5) * gain_ref[...]
        gated_ref[:, cols] = (normed * (gate * sigmoid(gate))).astype(LOW)


def mixer_forward(raw, keep, conv, rates, gain, heads):
    rows, width = raw.shape
    count = rows // STRETCH
    kw, vw = heads * DK, heads * DV
    qkv = 2 * kw + vw
    at = lambda n, keep_ref: (n, 0)
    fixed = lambda n, keep_ref: (0, 0)
    at4 = lambda n, keep_ref: (n, 0, 0, 0)
    spec = pl.BlockSpec
    return pl.pallas_call(
        functools.partial(forward_kernel, heads),
        grid_spec=pltpu.PrefetchScalarGridSpec(
            num_scalar_prefetch=1,
            grid=(count,),
            in_specs=[spec((STRETCH, width), at), spec((4, qkv), fixed), spec((HALO, LANES), fixed), spec((1, DV), fixed)],
            out_specs=[
                spec((STRETCH, vw), at),
                spec((STRETCH, qkv), at),
                spec((STRETCH, vw), at),
                spec((STRETCH, vw), at),
                spec((1, heads, STRETCH, STRETCH), at4),
                spec((1, heads, DK, DV), at4),
            ],
            scratch_shapes=[pltpu.VMEM((heads, DK, DV), F32), pltpu.VMEM((STRETCH + HALO, qkv), F32)],
        ),
        out_shape=[
            jax.ShapeDtypeStruct((rows, vw), LOW),
            jax.ShapeDtypeStruct((rows, qkv), F32),
            jax.ShapeDtypeStruct((rows, vw), F32),
            jax.ShapeDtypeStruct((rows, vw), F32),
            jax.ShapeDtypeStruct((count, heads, STRETCH, STRETCH), F32),
            jax.ShapeDtypeStruct((count, heads, DK, DV), F32),
        ],
        compiler_params=pltpu.CompilerParams(dimension_semantics=("arbitrary",), vmem_limit_bytes=32 << 20),
        cost_estimate=pl.CostEstimate(flops=1000, bytes_accessed=1000, transcendentals=0),
        name="mixer_forward",
    )(keep, raw, conv, rates, gain)


def backward_kernel(heads, keep_ref, raw_ref, conved_ref, fresh_ref, out_ref, inv_ref, start_ref, grad_ref,
                    conv_ref, rates_ref, gain_ref,
                    draw_ref, dconv_ref, drates_ref, dgain_ref, dstate, ext):
    i = pl.program_id(0)
    count = pl.num_programs(0)
    n = count - 1 - i
    keep_next = keep_ref[n + 1].astype(F32)
    kw, vw = heads * DK, heads * DV
    qkv = 2 * kw + vw
    span = STRETCH

    @pl.when(i == 0)
    def _():
        dstate[...] = jnp.zeros_like(dstate)
        ext[...] = jnp.zeros_like(ext)
        dconv_ref[...] = jnp.zeros_like(dconv_ref)
        drates_ref[...] = jnp.zeros_like(drates_ref)
        dgain_ref[...] = jnp.zeros_like(dgain_ref)

    ext[span:span + HALO, :] = ext[0:HALO, :] * keep_next
    rates = rates_ref[...]
    mixed = raw_ref[:, qkv + vw:]
    decay, soft_in, sum_col, sum_row = decay_parts(mixed, rates, heads)
    beta_all = sigmoid(mixed)
    row, col = block_masks()
    incl, strict = row >= col, row > col
    lane = lax.broadcasted_iota(jnp.int32, (span, LANES), 1)
    last_row = lax.broadcasted_iota(jnp.int32, (span, 1), 0) == span - 1
    gain = gain_ref[...]
    dgain = jnp.zeros((1, DV), F32)
    dsum_all = jnp.zeros((span, LANES), F32)
    dbeta_all = jnp.zeros((span, LANES), F32)
    down_rows = []

    def act(begin, width):
        c = conved_ref[:, begin:begin + width]
        s = sigmoid(c)
        return c * s, s * (1.0 + c * (1.0 - s))

    for h in range(heads):
        cols = slice(h * DV, (h + 1) * DV)
        zq, slope_q = act(h * DK, DK)
        zk, slope_k = act(kw + h * DK, DK)
        v, slope_v = act(2 * kw + h * DV, DV)
        rq = lax.rsqrt(jnp.sum(zq * zq, axis=-1, keepdims=True) + 1e-6)
        rk = lax.rsqrt(jnp.sum(zk * zk, axis=-1, keepdims=True) + 1e-6)
        q = zq * rq * DK ** -0.5
        k = zk * rk
        within = jnp.exp(jnp.where(incl, sum_col[:, h:h + 1] - sum_row[h:h + 1, :], -1e30))
        beta = beta_all[:, heads + h:heads + h + 1]
        total = sum_col[:, h:h + 1]
        growth = jnp.exp(total)
        last = total[span - 1:span, :]
        growth_last = jnp.exp(last)
        tail = jnp.exp(last - total)
        start = start_ref[0, h].astype(F32)
        fresh = fresh_ref[:, cols].astype(F32)
        inv = inv_ref[0, h]
        scores = mm(q, k, NT, 3) * within
        inner = mm(k, k, NT, 3)
        k_state = mm(k, start, NN, 3)
        q_state = mm(q, start, NN, 3)
        out = out_ref[:, cols]
        gate = raw_ref[:, qkv + h * DV:qkv + (h + 1) * DV]
        gate_sig = sigmoid(gate)
        gate_act = gate * gate_sig
        dgated = grad_ref[:, cols].astype(F32)
        r = lax.rsqrt(jnp.mean(out * out, axis=-1, keepdims=True) + 1e-5)
        unit = out * r
        dnormed = dgated * gate_act
        draw_ref[:, qkv + h * DV:qkv + (h + 1) * DV] = (
            dgated * (unit * gain) * (gate_sig * (1.0 + gate * (1.0 - gate_sig)))
        ).astype(LOW)
        dgain = dgain + jnp.sum(dnormed * unit, axis=0, keepdims=True)
        dunit = dnormed * gain
        dout = r * (dunit - unit * jnp.mean(dunit * unit, axis=-1, keepdims=True))
        dnext = dstate[h] * keep_next
        dfresh = mm(scores, dout, TN, 1) + mm(k * tail, dnext, NN, 1)
        dright = mm(inv, dfresh, TN, 1)
        dscores = jnp.where(incl, mm(dout, fresh, NT, 1), 0.0)
        dlower = jnp.where(strict, -mm(dright, fresh, NT, 1), 0.0)
        scaled = beta * growth * dright
        dstate[h] = growth_last * dnext + mm(q * growth, dout, TN, 1) - mm(k, scaled, TN, 1)
        dv = beta * dright
        dbeta = jnp.sum(dright * (v - growth * k_state), axis=-1, keepdims=True)
        dgrowth = jnp.sum(dout * q_state - dv * k_state, axis=-1, keepdims=True)
        dsw = dscores * within
        dq = growth * mm(dout, start, NT, 1) + mm(dsw, k, NN, 1)
        into_k = mm(fresh, dnext, NT, 1)
        dinner = dlower * within
        dbeta = dbeta + jnp.sum(dinner * inner, axis=-1, keepdims=True)
        weighted = beta * dinner
        dk = (
            tail * into_k
            - mm(scaled, start, NT, 1)
            + mm(dsw, q, TN, 1)
            + mm(weighted, k, NN, 1)
            + mm(weighted, k, TN, 1)
        )
        tailed = tail * jnp.sum(k * into_k, axis=-1, keepdims=True)
        pairs = dscores * scores + weighted * inner
        at_last = growth_last * jnp.sum(start * dnext, keepdims=True) + jnp.sum(tailed, keepdims=True)
        dsum = jnp.sum(pairs, axis=-1, keepdims=True) + growth * dgrowth - tailed + jnp.where(last_row, at_last, 0.0)
        down_rows.append(jnp.sum(pairs, axis=0, keepdims=True))
        dsum_all = jnp.where(lane == h, dsum, dsum_all)
        dbeta_all = jnp.where(lane == heads + h, dbeta, dbeta_all)
        dzq = (DK ** -0.5 * rq) * (dq - zq * (rq * rq * jnp.sum(dq * zq, axis=-1, keepdims=True)))
        dzk = rk * (dk - zk * (rk * rk * jnp.sum(dk * zk, axis=-1, keepdims=True)))
        ext[0:span, h * DK:(h + 1) * DK] = dzq * slope_q
        ext[0:span, kw + h * DK:kw + (h + 1) * DK] = dzk * slope_k
        ext[0:span, 2 * kw + h * DV:2 * kw + (h + 1) * DV] = dv * slope_v

    dgain_ref[...] += dgain
    upper = jnp.where(row <= col, 1.0, 0.0)
    down = jnp.concatenate(down_rows + [jnp.zeros((LANES - heads, span), F32)], axis=0)
    ddecay = mm(upper, dsum_all, NN, 6) - mm(upper, down, NT, 6)
    ddecay = jnp.where(lane < heads, ddecay, 0.0)
    dalpha = ddecay * (-jnp.exp(rates[0:1, :])) * sigmoid(soft_in)
    dbeta_raw = jnp.where((lane >= heads) & (lane < 2 * heads), dbeta_all * beta_all * (1.0 - beta_all), 0.0)
    draw_ref[:, qkv + vw:] = (dalpha + dbeta_raw).astype(LOW)
    drates_ref[0:1, :] += jnp.sum(ddecay * decay, axis=0, keepdims=True)
    drates_ref[1:2, :] += jnp.sum(dalpha, axis=0, keepdims=True)
    wide = 256
    for begin in range(0, qkv, wide):
        cols = slice(begin, begin + wide)
        raw = raw_ref[:, cols]
        total = None
        for j in range(4):
            shifted = ext[j:j + span, cols]
            term = shifted * conv_ref[j:j + 1, cols]
            total = term if total is None else total + term
            dconv_ref[j:j + 1, cols] += jnp.sum(raw * shifted, axis=0, keepdims=True)
        draw_ref[:, cols] = total.astype(LOW)


def mixer_backward(raw, kept, grad, keep, conv, rates, gain, heads):
    conved, fresh, out, inv, start = kept
    rows, width = raw.shape
    count = rows // STRETCH
    kw, vw = heads * DK, heads * DV
    qkv = 2 * kw + vw
    at = lambda i, keep_ref: (count - 1 - i, 0)
    fixed = lambda i, keep_ref: (0, 0)
    at4 = lambda i, keep_ref: (count - 1 - i, 0, 0, 0)
    spec = pl.BlockSpec
    return pl.pallas_call(
        functools.partial(backward_kernel, heads),
        grid_spec=pltpu.PrefetchScalarGridSpec(
            num_scalar_prefetch=1,
            grid=(count,),
            in_specs=[
                spec((STRETCH, width), at),
                spec((STRETCH, qkv), at),
                spec((STRETCH, vw), at),
                spec((STRETCH, vw), at),
                spec((1, heads, STRETCH, STRETCH), at4),
                spec((1, heads, DK, DV), at4),
                spec((STRETCH, vw), at),
                spec((4, qkv), fixed),
                spec((HALO, LANES), fixed),
                spec((1, DV), fixed),
            ],
            out_specs=[spec((STRETCH, width), at), spec((4, qkv), fixed), spec((HALO, LANES), fixed), spec((1, DV), fixed)],
            scratch_shapes=[pltpu.VMEM((heads, DK, DV), F32), pltpu.VMEM((STRETCH + HALO, qkv), F32)],
        ),
        out_shape=[
            jax.ShapeDtypeStruct((rows, width), LOW),
            jax.ShapeDtypeStruct((4, qkv), F32),
            jax.ShapeDtypeStruct((HALO, LANES), F32),
            jax.ShapeDtypeStruct((1, DV), F32),
        ],
        compiler_params=pltpu.CompilerParams(dimension_semantics=("arbitrary",), vmem_limit_bytes=32 << 20),
        cost_estimate=pl.CostEstimate(flops=1000, bytes_accessed=1000, transcendentals=0),
        name="mixer_backward",
    )(jnp.concatenate([keep, jnp.zeros((1,), jnp.int32)]), raw, conved, fresh, out, inv, start, grad, conv, rates, gain)


def product(left_rows, matrix):
    return lax.dot_general(left_rows, matrix, NN, preferred_element_type=F32)


def product_nt(left_rows, matrix):
    return lax.dot_general(left_rows, matrix, NT, preferred_element_type=F32)


def product_tn(left_rows, right_rows):
    return lax.dot_general(left_rows, right_rows, TN, preferred_element_type=F32)


def rms_rows(rows_in, gain_row):
    return (
        rows_in * lax.rsqrt(jnp.mean(rows_in * rows_in, axis=-1, keepdims=True) + 1e-06) * gain_row
    )


def layout(pack_lengths, pack_rows):
    positions = jnp.arange(pack_rows, dtype=jnp.int32)
    first_len = pack_lengths[0]
    second_len = pack_lengths[1]
    second_start = (first_len + STRETCH - 1) // STRETCH * STRETCH
    live_rows = (positions < first_len) | (positions >= second_start) & (
        positions < second_start + second_len
    )
    stretch_starts = jnp.arange(pack_rows // STRETCH, dtype=jnp.int32) * STRETCH
    keep_state = jnp.where(
        (stretch_starts == 0) | (stretch_starts == second_start), 0, 1
    ).astype(jnp.int32)
    return (keep_state, jnp.where(live_rows, 1.0, 0.0).astype(jnp.float32))


def rotation(count, shift):
    return [(i, (i + shift) % count) for i in range(count)]


def hold(*values):
    return lax.optimization_barrier(values)


def place_slots(found, axis):
    count = len(found)
    t = lax.axis_index("tensor")
    slots = []
    for slot in range(count):
        ahead = jnp.where(slot < t, slot - t + count, slot - t)
        chosen = found[0]
        for shift in range(1, count):
            chosen = jnp.where(ahead == shift, found[shift], chosen)
        slots.append(chosen)
    return jnp.concatenate(slots, axis=axis)


def z_fetch(own):
    count = lax.axis_size("tensor")
    return [own] + [
        lax.ppermute(own, "tensor", rotation(count, -shift)) for shift in range(1, count)
    ]


def queued_gather(own):
    return lax.all_gather(own, "tensor", axis=0, tiled=True)


def queued_scatter(partial):
    return lax.psum_scatter(
        partial.astype(jnp.bfloat16), "tensor", scatter_dimension=0, tiled=True
    )


def z_terms(partial):
    count = lax.axis_size("tensor")
    t = lax.axis_index("tensor")
    rows = partial.shape[0] // count
    parts = partial.reshape(count, rows, partial.shape[1])

    def take(ahead):
        index = jnp.where(t + ahead < count, t + ahead, t + ahead - count)
        return lax.dynamic_index_in_dim(parts, index, 0, keepdims=False)

    return take(0), [take(shift).astype(jnp.bfloat16) for shift in range(1, count)]


def z_ship(terms):
    count = lax.axis_size("tensor")
    return [
        lax.ppermute(term, "tensor", rotation(count, shift + 1)) for shift, term in enumerate(terms)
    ]


def z_sum(own, sent):
    for term in sent:
        own = own + term.astype(jnp.float32)
    return own


def relay_near(own):
    if lax.axis_size("tensor") != 4:
        return tuple(z_fetch(own))
    right = lax.ppermute(own, "tensor", [(0, 1), (1, 2), (2, 3)])
    left = lax.ppermute(own, "tensor", [(1, 0), (2, 1), (3, 2)])
    return own, right, left


def relay_far(near, axis):
    if lax.axis_size("tensor") != 4:
        return place_slots(near, axis)
    own, right, left = near
    t = lax.axis_index("tensor")
    right2 = lax.ppermute(right, "tensor", [(1, 2), (2, 3)])
    left2 = lax.ppermute(left, "tensor", [(1, 0), (2, 1)])
    far = lax.ppermute(jnp.where(t == 1, right, left), "tensor", [(1, 3), (2, 0)])

    def pick(a, b, c, d):
        return jnp.where(t == 0, a, jnp.where(t == 1, b, jnp.where(t == 2, c, d)))

    return jnp.concatenate(
        [
            pick(own, right, right2, far),
            pick(left, own, right, right2),
            pick(left2, left, own, right),
            pick(far, left2, left, own),
        ],
        axis=axis,
    )


def sum_over(values, axis):
    count = lax.axis_size(axis)
    if count & (count - 1):
        return lax.psum(values, axis)
    step = 1
    while step < count:
        values = values + lax.ppermute(values, axis, [(i, i ^ step) for i in range(count)])
        step *= 2
    return values


def gather_rows(local):
    return lax.all_gather(local, "dp", axis=0, tiled=True)


def scatter_rows(partial):
    return lax.psum_scatter(
        partial.astype(jnp.bfloat16), "dp", scatter_dimension=0, tiled=True
    ).astype(jnp.float32)


def shards(
    tokens,
    lengths,
    mixer_gain,
    query_weight,
    key_weight,
    value_weight,
    outgate_weight,
    alpha_weight,
    beta_weight,
    query_conv,
    key_conv,
    value_conv,
    log_rate,
    rate_bias,
    head_gain,
    output_weight,
    feed_gain,
    gate_weight,
    up_weight,
    down_weight,
    cotangent,
):
    tensor_index = lax.axis_index("tensor")
    tensor_count = lax.axis_size("tensor")
    micro_count, local_rows, width = tokens.shape
    pack_rows = local_rows * tensor_count
    key_width = query_weight.shape[1]
    value_width = value_weight.shape[1]
    head_count = alpha_weight.shape[1]
    hidden_width = gate_weight.shape[1]
    low = jnp.bfloat16

    edges = (key_width, 2 * key_width, 2 * key_width + value_width, 2 * key_width + 2 * value_width)
    pad = -(2 * head_count) % LANES
    in_local = jnp.concatenate(
        [
            query_weight,
            key_weight,
            value_weight,
            outgate_weight,
            alpha_weight,
            beta_weight,
            jnp.zeros((query_weight.shape[0], pad), low),
        ],
        axis=1,
    )
    in_full = gather_rows(in_local)
    out_full = gather_rows(output_weight.T)
    feed_full = gather_rows(jnp.concatenate([gate_weight, up_weight], axis=1))
    down_full = gather_rows(down_weight.T)

    small_local = (
        lax.dynamic_slice_in_dim(query_conv, tensor_index * key_width, key_width, 1),
        lax.dynamic_slice_in_dim(key_conv, tensor_index * key_width, key_width, 1),
        lax.dynamic_slice_in_dim(value_conv, tensor_index * value_width, value_width, 1),
        lax.dynamic_slice_in_dim(log_rate, tensor_index * head_count, head_count, 0),
        lax.dynamic_slice_in_dim(rate_bias, tensor_index * head_count, head_count, 0),
        head_gain,
    )
    packs = range(micro_count)
    wide = jnp.float32
    token_rows = [tokens[m].astype(wide) for m in packs]
    layouts = [layout(lengths[m, 0], pack_rows) for m in packs]
    own_masks = [
        lax.dynamic_slice_in_dim(row_mask, tensor_index * local_rows, local_rows, 0)[:, None]
        for _, row_mask in layouts
    ]
    out_grads = [cotangent[m].astype(wide) * own_masks[m] for m in packs]
    norm_ones = [jax.vjp(rms_rows, token_rows[m], mixer_gain) for m in packs]
    conv_local = jnp.concatenate(small_local[:3], axis=1)
    rates = jnp.zeros((HALO, LANES), wide)
    rates = rates.at[0, :head_count].set(small_local[3]).at[1, :head_count].set(small_local[4])
    gain_row = head_gain[None, :]
    joined = lambda *parts: jnp.concatenate(parts, axis=0)

    def mix(m, raw):
        mixed, *rest = mixer_forward(raw, layouts[m][0], conv_local, rates, gain_row, head_count)
        return mixed, rest

    def settle(m, received):
        middle = token_rows[m] + received.astype(wide)
        normed, back = jax.vjp(rms_rows, middle, feed_gain)
        return middle, normed.astype(low), back

    def feed_forward(second, hidden_grad):
        pre = product(second, feed_full)
        gate_pre, up_pre = pre[:, :hidden_width], pre[:, hidden_width:]
        gate_sig = jax.nn.sigmoid(gate_pre)
        gate_act = gate_pre * gate_sig
        hidden = (gate_act * up_pre).astype(low)
        gate_grad = hidden_grad * up_pre * gate_sig * (1.0 + gate_pre * (1.0 - gate_sig))
        feed_grad = jnp.concatenate([gate_grad, hidden_grad * gate_act], axis=1).astype(low)
        return hidden, feed_grad, product_nt(feed_grad, feed_full).astype(low)

    def feed_back(m, back, received):
        norm_grad, gain_grad = back(received.astype(wide))
        total = out_grads[m] + norm_grad
        return total, total.astype(low), gain_grad

    def mix_back(m, rows_in, raw, rest):
        return mixer_backward(
            raw, rest, product(rows_in, out_full), layouts[m][0], conv_local, rates, gain_row, head_count
        )

    A, B = 0, 1
    first_own = jnp.stack([norm_ones[m][0].astype(low) for m in packs])
    grad_own = jnp.stack([out_grads[m].astype(low) for m in packs])
    first_all = relay_far(relay_near(first_own), 1)
    first_all, in_full, grad_own = hold(first_all, in_full, grad_own)
    first_a, first_b = first_all[A], first_all[B]
    grad_near = relay_near(grad_own)
    raw_a = product(first_a, in_full)
    mixed_a, rest_a = mix(A, raw_a)
    mixed_a, *grad_near = hold(mixed_a, *grad_near)
    own_a, terms_a = z_terms(product_nt(mixed_a, out_full))
    sent_a = z_ship(terms_a)
    grad_all = relay_far(grad_near, 1)
    grad_a, grad_b = grad_all[A], grad_all[B]
    first_b, own_a = hold(first_b, own_a)
    raw_b = product(first_b, in_full)
    mixed_b, rest_b = mix(B, raw_b)
    mixed_b, own_a, feed_full, down_full, *sent_a = hold(
        mixed_b, own_a, feed_full, down_full, *sent_a
    )
    middle_a, normed_a, back_a = settle(A, z_sum(own_a, sent_a))
    second_a = queued_gather(normed_a)
    part_b = product_nt(mixed_b, out_full).astype(low)
    grad_a, grad_b, part_b = hold(grad_a, grad_b, part_b)
    hidden_grad_a = product(grad_a, down_full)
    hidden_grad_b = product(grad_b, down_full)
    second_a, part_b, hidden_grad_a, hidden_grad_b = hold(
        second_a, part_b, hidden_grad_a, hidden_grad_b
    )
    sum_b = queued_scatter(part_b)
    hidden_a, feed_grad_a, part2_a = feed_forward(second_a, hidden_grad_a)
    part2_a, sum_b = hold(part2_a, sum_b)
    sum2_a = queued_scatter(part2_a)
    middle_b, normed_b, back_b = settle(B, sum_b)
    result_a = z_terms(product_nt(hidden_a, down_full))
    normed_b, sum2_a, result_own = hold(normed_b, sum2_a, result_a[0])
    result_a = (result_own, result_a[1])
    second_b = queued_gather(normed_b)
    middle_grad_a, low_a, gain_grad_a = feed_back(A, back_a, sum2_a)
    low_a, second_b = hold(low_a, second_b)
    mix_rows_a = queued_gather(low_a)
    hidden_b, feed_grad_b, part2_b = feed_forward(second_b, hidden_grad_b)
    part2_b, mix_rows_a = hold(part2_b, mix_rows_a)
    sum2_b = queued_scatter(part2_b)
    result_b = z_terms(product_nt(hidden_b, down_full))
    feed_grad = product_tn(joined(second_a, second_b), joined(feed_grad_a, feed_grad_b)).astype(low)
    down_grad = product_tn(joined(grad_a, grad_b), joined(hidden_a, hidden_b)).astype(low)
    both_grad = jnp.concatenate([feed_grad, down_grad], axis=1)
    both_grad, sum2_b, mix_rows_a, result_own = hold(both_grad, sum2_b, mix_rows_a, result_b[0])
    result_b = (result_own, result_b[1])
    feed_width = 2 * hidden_width
    both_final = scatter_rows(both_grad)
    middle_grad_b, low_b, gain_grad_b = feed_back(B, back_b, sum2_b)
    mix_found_b = z_fetch(low_b)
    raw_grad_a, *core_a = mix_back(A, mix_rows_a, raw_a, rest_a)
    raw_grad_a, *mix_found_b = hold(raw_grad_a, *mix_found_b)
    mix_rows_b = place_slots(mix_found_b, 0)
    mix_rows_b, *final_terms = hold(mix_rows_b, *result_a[1])
    split_at = len(final_terms)
    final_a = (result_a[0], z_ship(final_terms))
    raw_grad_b, *core_b = mix_back(B, mix_rows_b, raw_b, rest_b)
    raw_grad_b, raw_grad_a, mixed_a, final_own, *sent_final = hold(
        raw_grad_b, raw_grad_a, mixed_a, final_a[0], *final_a[1]
    )
    final_a = (final_own, sent_final)
    raw_grad_b, *moved = hold(raw_grad_b, *result_b[1])
    final_b = (result_b[0], z_ship(moved))
    in_grad = product_tn(joined(first_a, first_b), joined(raw_grad_a, raw_grad_b)).astype(low)
    out_grad = product_tn(joined(mix_rows_a, mix_rows_b), joined(mixed_a, mixed_b)).astype(low)
    in_grad = jnp.concatenate([in_grad, out_grad], axis=1)
    raw_grad_a, in_grad, both_final = hold(raw_grad_a, in_grad, both_final)
    part3_a = product_nt(raw_grad_a, in_full)
    own3_a, terms3_a = z_terms(part3_a)
    sent3_a = z_ship(terms3_a)
    last_final = scatter_rows(in_grad)
    in_final, out_final = last_final[:, : in_full.shape[1]], last_final[:, in_full.shape[1] :]
    part3_b = product_nt(raw_grad_b, in_full)
    own3_b, terms3_b = z_terms(part3_b)
    sent3_b = z_ship(terms3_b)
    outputs = [
        ((middle_a + z_sum(*final_a)) * own_masks[A]).astype(low),
        ((middle_b + z_sum(*final_b)) * own_masks[B]).astype(low),
    ]
    token_grad_a = norm_ones[A][1](z_sum(own3_a, sent3_a))[0]
    token_grad_b = norm_ones[B][1](z_sum(own3_b, sent3_b))[0]
    mixer_gain_grad = (
        jnp.sum(part3_a * first_a.astype(wide), axis=0)
        + jnp.sum(part3_b * first_b.astype(wide), axis=0)
    ) / mixer_gain
    input_grads = [middle_grad_a + token_grad_a, middle_grad_b + token_grad_b]
    feed_gain_grad = gain_grad_a + gain_grad_b
    conv_grads, rate_grads, gain_grads = [x + y for x, y in zip(core_a, core_b)]
    rate_grads, gain_grads = rate_grads[:2, :head_count], gain_grads[0]
    everywhere = jnp.concatenate([feed_gain_grad, mixer_gain_grad, gain_grads])
    per_slice = jnp.concatenate([conv_grads.reshape(-1), rate_grads.reshape(-1)])
    packed = sum_over(jnp.concatenate([per_slice, everywhere]), "dp")
    slices = jnp.zeros((tensor_count, per_slice.size), wide)
    slices = lax.dynamic_update_index_in_dim(slices, packed[: per_slice.size], tensor_index, 0)
    packed = sum_over(jnp.concatenate([slices.reshape(-1), packed[per_slice.size :]]), "tensor")
    slices = packed[: slices.size].reshape(tensor_count, per_slice.size)
    taps = query_conv.shape[0]
    conv_all = slices[:, : conv_grads.size].reshape(tensor_count, taps, -1)

    def all_columns(begin, end):
        return jnp.moveaxis(conv_all[:, :, begin:end], 0, 1).reshape(taps, -1)

    rate_all = slices[:, conv_grads.size :]
    everywhere = packed[slices.size :]
    return (
        jnp.stack(outputs),
        jnp.stack(input_grads),
        everywhere[width : 2 * width],
        in_final[:, : edges[0]],
        in_final[:, edges[0] : edges[1]],
        in_final[:, edges[1] : edges[2]],
        in_final[:, edges[2] : edges[3]],
        in_final[:, edges[3] : edges[3] + head_count],
        in_final[:, edges[3] + head_count : edges[3] + 2 * head_count],
        all_columns(0, edges[0]),
        all_columns(edges[0], edges[1]),
        all_columns(edges[1], edges[2]),
        rate_all[:, :head_count].reshape(-1),
        rate_all[:, head_count:].reshape(-1),
        everywhere[2 * width :],
        out_final.T,
        everywhere[:width],
        both_final[:, :hidden_width],
        both_final[:, hidden_width:feed_width],
        both_final[:, feed_width:].T,
    )


def solution(mesh):
    return jax.shard_map(
        shards,
        mesh=mesh,
        in_specs=(
            P(None, ("dp", "tensor"), None),
            P(None, "dp", None),
            P(),
            P("dp", "tensor"),
            P("dp", "tensor"),
            P("dp", "tensor"),
            P("dp", "tensor"),
            P("dp", "tensor"),
            P("dp", "tensor"),
            P(),
            P(),
            P(),
            P(),
            P(),
            P(),
            P("tensor", "dp"),
            P(),
            P("dp", "tensor"),
            P("dp", "tensor"),
            P("tensor", "dp"),
            P(None, ("dp", "tensor"), None),
        ),
        out_specs=(
            P(None, ("dp", "tensor"), None),
            P(None, ("dp", "tensor"), None),
            P(),
            P("dp", "tensor"),
            P("dp", "tensor"),
            P("dp", "tensor"),
            P("dp", "tensor"),
            P("dp", "tensor"),
            P("dp", "tensor"),
            P(),
            P(),
            P(),
            P(),
            P(),
            P(),
            P("tensor", "dp"),
            P(),
            P("dp", "tensor"),
            P("dp", "tensor"),
            P("tensor", "dp"),
        ),
        check_vma=False,
    )
```

```python
import functools
import jax
import jax.numpy as jnp
from jax import lax
from jax.experimental import pallas as pl
from jax.experimental.pallas import tpu as pltpu
from jax.sharding import PartitionSpec as P

DK = 128
DV = 256
STRETCH = 64
LANES = 128
HALO = 8
F32 = jnp.float32
LOW = jnp.bfloat16

NN = (((1,), (0,)), ((), ()))
NT = (((1,), (1,)), ((), ()))
TN = (((0,), (0,)), ((), ()))


def split(a):
    hi = a.astype(LOW)
    return hi, (a - hi.astype(F32)).astype(LOW)


def mm(a, b, dims=NN, passes=1):
    if passes == 6:
        return lax.dot_general(a, b, dims, precision=lax.Precision.HIGHEST, preferred_element_type=F32)
    dot = functools.partial(lax.dot_general, dimension_numbers=dims, preferred_element_type=F32)
    if passes == 1:
        return dot(a.astype(LOW), b.astype(LOW))
    ah, al = split(a)
    bh, bl = split(b)
    return dot(ah, bh) + (dot(ah, bl) + dot(al, bh))


def block_masks():
    row = lax.broadcasted_iota(jnp.int32, (STRETCH, STRETCH), 0)
    col = lax.broadcasted_iota(jnp.int32, (STRETCH, STRETCH), 1)
    return row, col


def sigmoid(v):
    return 1.0 / (1.0 + jnp.exp(-v))


def softplus(v):
    return jnp.maximum(v, 0.0) + jnp.log1p(jnp.exp(-jnp.abs(v)))


def unit_inverses(lowers, passes):
    row, col = block_masks()
    eye = jnp.where(row == col, 1.0, 0.0)
    pair = (row // 2 == col // 2) & (row > col)
    inverses = [eye - jnp.where(pair, lower, 0.0) for lower in lowers]
    size = 2
    while size < STRETCH:
        off = (row // (2 * size) == col // (2 * size)) & (row // size > col // size)
        offs = [jnp.where(off, lower, 0.0) for lower in lowers]
        halves = [mm(inv, o, NN, passes) for inv, o in zip(inverses, offs)]
        inverses = [inv - mm(h, inv, NN, passes) for inv, h in zip(inverses, halves)]
        size *= 2
    return inverses


def decay_parts(mixed, rates, heads):
    lane = lax.broadcasted_iota(jnp.int32, (STRETCH, LANES), 1)
    row, col = block_masks()
    soft_in = mixed + rates[1:2, :]
    decay = jnp.where(lane < heads, -jnp.exp(rates[0:1, :]) * softplus(soft_in), 0.0)
    tri = jnp.where(row >= col, 1.0, 0.0)
    upper = jnp.where(row <= col, 1.0, 0.0)
    sum_col = mm(tri, decay, NN, 6)
    sum_row = mm(decay[:, :HALO], upper, TN, 6)
    return decay, soft_in, sum_col, sum_row


def forward_kernel(heads, keep_ref, raw_ref, conv_ref, rates_ref, gain_ref,
                   gated_ref, conved_ref, fresh_ref, out_ref, inv_ref, start_ref, state, ext):
    n = pl.program_id(0)
    keep = keep_ref[n].astype(F32)
    kw, vw = heads * DK, heads * DV
    qkv = 2 * kw + vw
    span = STRETCH

    @pl.when(n == 0)
    def _():
        state[...] = jnp.zeros_like(state)
        ext[...] = jnp.zeros_like(ext)

    ext[0:HALO, :] = ext[span:span + HALO, :] * keep
    ext[HALO:HALO + span, :] = raw_ref[:, :qkv]

    def conv(begin, width):
        total = ext[HALO:HALO + span, begin:begin + width] * conv_ref[0:1, begin:begin + width]
        for j in range(1, 4):
            total = total + ext[HALO - j:HALO - j + span, begin:begin + width] * conv_ref[j:j + 1, begin:begin + width]
        conved_ref[:, begin:begin + width] = total
        return total * sigmoid(total)

    mixed = raw_ref[:, qkv + vw:]
    decay, _, sum_col, sum_row = decay_parts(mixed, rates_ref[...], heads)
    beta_all = sigmoid(mixed)
    row, col = block_masks()
    incl, strict = row >= col, row > col
    qs, ks, lowers, scores, betas = [], [], [], [], []
    for h in range(heads):
        zq = conv(h * DK, DK)
        zk = conv(kw + h * DK, DK)
        q = zq * lax.rsqrt(jnp.sum(zq * zq, axis=-1, keepdims=True) + 1e-6) * DK ** -0.5
        k = zk * lax.rsqrt(jnp.sum(zk * zk, axis=-1, keepdims=True) + 1e-6)
        within = jnp.exp(jnp.where(incl, sum_col[:, h:h + 1] - sum_row[h:h + 1, :], -1e30))
        beta = beta_all[:, heads + h:heads + h + 1]
        scores.append(mm(q, k, NT, 3) * within)
        lowers.append(jnp.where(strict, beta * mm(k, k, NT, 3) * within, 0.0))
        qs.append(q); ks.append(k); betas.append(beta)
    inverses = unit_inverses(lowers, 3)
    for h in range(heads):
        q, k, beta = qs[h], ks[h], betas[h]
        start = state[h] * keep
        total = sum_col[:, h:h + 1]
        growth = jnp.exp(total)
        last = total[span - 1:span, :]
        v = conv(2 * kw + h * DV, DV)
        k_state = mm(k, start, NN, 3)
        q_state = mm(q, start, NN, 3)
        fresh = mm(inverses[h], beta * (v - growth * k_state), NN, 3)
        out = growth * q_state + mm(scores[h], fresh, NN, 3)
        tail = jnp.exp(last - total)
        state[h] = jnp.exp(last) * start + mm(k * tail, fresh, TN, 3)
        cols = slice(h * DV, (h + 1) * DV)
        fresh_ref[:, cols] = fresh.astype(fresh_ref.dtype)
        out_ref[:, cols] = out
        inv_ref[0, h] = inverses[h].astype(inv_ref.dtype)
        start_ref[0, h] = start.astype(start_ref.dtype)
        gate = raw_ref[:, qkv + h * DV:qkv + (h + 1) * DV]
        normed = out * lax.rsqrt(jnp.mean(out * out, axis=-1, keepdims=True) + 1e-5) * gain_ref[...]
        gated_ref[:, cols] = (normed * (gate * sigmoid(gate))).astype(LOW)


def mixer_forward(raw, keep, conv, rates, gain, heads):
    rows, width = raw.shape
    count = rows // STRETCH
    kw, vw = heads * DK, heads * DV
    qkv = 2 * kw + vw
    at = lambda n, keep_ref: (n, 0)
    fixed = lambda n, keep_ref: (0, 0)
    at4 = lambda n, keep_ref: (n, 0, 0, 0)
    spec = pl.BlockSpec
    return pl.pallas_call(
        functools.partial(forward_kernel, heads),
        grid_spec=pltpu.PrefetchScalarGridSpec(
            num_scalar_prefetch=1,
            grid=(count,),
            in_specs=[spec((STRETCH, width), at), spec((4, qkv), fixed), spec((HALO, LANES), fixed), spec((1, DV), fixed)],
            out_specs=[
                spec((STRETCH, vw), at),
                spec((STRETCH, qkv), at),
                spec((STRETCH, vw), at),
                spec((STRETCH, vw), at),
                spec((1, heads, STRETCH, STRETCH), at4),
                spec((1, heads, DK, DV), at4),
            ],
            scratch_shapes=[pltpu.VMEM((heads, DK, DV), F32), pltpu.VMEM((STRETCH + HALO, qkv), F32)],
        ),
        out_shape=[
            jax.ShapeDtypeStruct((rows, vw), LOW),
            jax.ShapeDtypeStruct((rows, qkv), F32),
            jax.ShapeDtypeStruct((rows, vw), F32),
            jax.ShapeDtypeStruct((rows, vw), F32),
            jax.ShapeDtypeStruct((count, heads, STRETCH, STRETCH), F32),
            jax.ShapeDtypeStruct((count, heads, DK, DV), F32),
        ],
        compiler_params=pltpu.CompilerParams(dimension_semantics=("arbitrary",), vmem_limit_bytes=32 << 20),
        cost_estimate=pl.CostEstimate(flops=1000, bytes_accessed=1000, transcendentals=0),
        name="mixer_forward",
    )(keep, raw, conv, rates, gain)


def backward_kernel(heads, keep_ref, raw_ref, conved_ref, fresh_ref, out_ref, inv_ref, start_ref, grad_ref,
                    conv_ref, rates_ref, gain_ref,
                    draw_ref, dconv_ref, drates_ref, dgain_ref, dstate, ext):
    i = pl.program_id(0)
    count = pl.num_programs(0)
    n = count - 1 - i
    keep_next = keep_ref[n + 1].astype(F32)
    kw, vw = heads * DK, heads * DV
    qkv = 2 * kw + vw
    span = STRETCH

    @pl.when(i == 0)
    def _():
        dstate[...] = jnp.zeros_like(dstate)
        ext[...] = jnp.zeros_like(ext)
        dconv_ref[...] = jnp.zeros_like(dconv_ref)
        drates_ref[...] = jnp.zeros_like(drates_ref)
        dgain_ref[...] = jnp.zeros_like(dgain_ref)

    ext[span:span + HALO, :] = ext[0:HALO, :] * keep_next
    rates = rates_ref[...]
    mixed = raw_ref[:, qkv + vw:]
    decay, soft_in, sum_col, sum_row = decay_parts(mixed, rates, heads)
    beta_all = sigmoid(mixed)
    row, col = block_masks()
    incl, strict = row >= col, row > col
    lane = lax.broadcasted_iota(jnp.int32, (span, LANES), 1)
    last_row = lax.broadcasted_iota(jnp.int32, (span, 1), 0) == span - 1
    gain = gain_ref[...]
    dgain = jnp.zeros((1, DV), F32)
    dsum_all = jnp.zeros((span, LANES), F32)
    dbeta_all = jnp.zeros((span, LANES), F32)
    down_rows = []

    def act(begin, width):
        c = conved_ref[:, begin:begin + width]
        s = sigmoid(c)
        return c * s, s * (1.0 + c * (1.0 - s))

    for h in range(heads):
        cols = slice(h * DV, (h + 1) * DV)
        zq, slope_q = act(h * DK, DK)
        zk, slope_k = act(kw + h * DK, DK)
        v, slope_v = act(2 * kw + h * DV, DV)
        rq = lax.rsqrt(jnp.sum(zq * zq, axis=-1, keepdims=True) + 1e-6)
        rk = lax.rsqrt(jnp.sum(zk * zk, axis=-1, keepdims=True) + 1e-6)
        q = zq * rq * DK ** -0.5
        k = zk * rk
        within = jnp.exp(jnp.where(incl, sum_col[:, h:h + 1] - sum_row[h:h + 1, :], -1e30))
        beta = beta_all[:, heads + h:heads + h + 1]
        total = sum_col[:, h:h + 1]
        growth = jnp.exp(total)
        last = total[span - 1:span, :]
        growth_last = jnp.exp(last)
        tail = jnp.exp(last - total)
        start = start_ref[0, h].astype(F32)
        fresh = fresh_ref[:, cols].astype(F32)
        inv = inv_ref[0, h]
        scores = mm(q, k, NT, 3) * within
        inner = mm(k, k, NT, 3)
        k_state = mm(k, start, NN, 3)
        q_state = mm(q, start, NN, 3)
        out = out_ref[:, cols]
        gate = raw_ref[:, qkv + h * DV:qkv + (h + 1) * DV]
        gate_sig = sigmoid(gate)
        gate_act = gate * gate_sig
        dgated = grad_ref[:, cols].astype(F32)
        r = lax.rsqrt(jnp.mean(out * out, axis=-1, keepdims=True) + 1e-5)
        unit = out * r
        dnormed = dgated * gate_act
        draw_ref[:, qkv + h * DV:qkv + (h + 1) * DV] = (
            dgated * (unit * gain) * (gate_sig * (1.0 + gate * (1.0 - gate_sig)))
        ).astype(LOW)
        dgain = dgain + jnp.sum(dnormed * unit, axis=0, keepdims=True)
        dunit = dnormed * gain
        dout = r * (dunit - unit * jnp.mean(dunit * unit, axis=-1, keepdims=True))
        dnext = dstate[h] * keep_next
        dfresh = mm(scores, dout, TN, 1) + mm(k * tail, dnext, NN, 1)
        dright = mm(inv, dfresh, TN, 1)
        dscores = jnp.where(incl, mm(dout, fresh, NT, 1), 0.0)
        dlower = jnp.where(strict, -mm(dright, fresh, NT, 1), 0.0)
        scaled = beta * growth * dright
        dstate[h] = growth_last * dnext + mm(q * growth, dout, TN, 1) - mm(k, scaled, TN, 1)
        dv = beta * dright
        dbeta = jnp.sum(dright * (v - growth * k_state), axis=-1, keepdims=True)
        dgrowth = jnp.sum(dout * q_state - dv * k_state, axis=-1, keepdims=True)
        dsw = dscores * within
        dq = growth * mm(dout, start, NT, 1) + mm(dsw, k, NN, 1)
        into_k = mm(fresh, dnext, NT, 1)
        dinner = dlower * within
        dbeta = dbeta + jnp.sum(dinner * inner, axis=-1, keepdims=True)
        weighted = beta * dinner
        dk = (
            tail * into_k
            - mm(scaled, start, NT, 1)
            + mm(dsw, q, TN, 1)
            + mm(weighted, k, NN, 1)
            + mm(weighted, k, TN, 1)
        )
        tailed = tail * jnp.sum(k * into_k, axis=-1, keepdims=True)
        pairs = dscores * scores + weighted * inner
        at_last = growth_last * jnp.sum(start * dnext, keepdims=True) + jnp.sum(tailed, keepdims=True)
        dsum = jnp.sum(pairs, axis=-1, keepdims=True) + growth * dgrowth - tailed + jnp.where(last_row, at_last, 0.0)
        down_rows.append(jnp.sum(pairs, axis=0, keepdims=True))
        dsum_all = jnp.where(lane == h, dsum, dsum_all)
        dbeta_all = jnp.where(lane == heads + h, dbeta, dbeta_all)
        dzq = (DK ** -0.5 * rq) * (dq - zq * (rq * rq * jnp.sum(dq * zq, axis=-1, keepdims=True)))
        dzk = rk * (dk - zk * (rk * rk * jnp.sum(dk * zk, axis=-1, keepdims=True)))
        ext[0:span, h * DK:(h + 1) * DK] = dzq * slope_q
        ext[0:span, kw + h * DK:kw + (h + 1) * DK] = dzk * slope_k
        ext[0:span, 2 * kw + h * DV:2 * kw + (h + 1) * DV] = dv * slope_v

    dgain_ref[...] += dgain
    upper = jnp.where(row <= col, 1.0, 0.0)
    down = jnp.concatenate(down_rows + [jnp.zeros((LANES - heads, span), F32)], axis=0)
    ddecay = mm(upper, dsum_all, NN, 6) - mm(upper, down, NT, 6)
    ddecay = jnp.where(lane < heads, ddecay, 0.0)
    dalpha = ddecay * (-jnp.exp(rates[0:1, :])) * sigmoid(soft_in)
    dbeta_raw = jnp.where((lane >= heads) & (lane < 2 * heads), dbeta_all * beta_all * (1.0 - beta_all), 0.0)
    draw_ref[:, qkv + vw:] = (dalpha + dbeta_raw).astype(LOW)
    drates_ref[0:1, :] += jnp.sum(ddecay * decay, axis=0, keepdims=True)
    drates_ref[1:2, :] += jnp.sum(dalpha, axis=0, keepdims=True)
    wide = 256
    for begin in range(0, qkv, wide):
        cols = slice(begin, begin + wide)
        raw = raw_ref[:, cols]
        total = None
        for j in range(4):
            shifted = ext[j:j + span, cols]
            term = shifted * conv_ref[j:j + 1, cols]
            total = term if total is None else total + term
            dconv_ref[j:j + 1, cols] += jnp.sum(raw * shifted, axis=0, keepdims=True)
        draw_ref[:, cols] = total.astype(LOW)


def mixer_backward(raw, kept, grad, keep, conv, rates, gain, heads):
    conved, fresh, out, inv, start = kept
    rows, width = raw.shape
    count = rows // STRETCH
    kw, vw = heads * DK, heads * DV
    qkv = 2 * kw + vw
    at = lambda i, keep_ref: (count - 1 - i, 0)
    fixed = lambda i, keep_ref: (0, 0)
    at4 = lambda i, keep_ref: (count - 1 - i, 0, 0, 0)
    spec = pl.BlockSpec
    return pl.pallas_call(
        functools.partial(backward_kernel, heads),
        grid_spec=pltpu.PrefetchScalarGridSpec(
            num_scalar_prefetch=1,
            grid=(count,),
            in_specs=[
                spec((STRETCH, width), at),
                spec((STRETCH, qkv), at),
                spec((STRETCH, vw), at),
                spec((STRETCH, vw), at),
                spec((1, heads, STRETCH, STRETCH), at4),
                spec((1, heads, DK, DV), at4),
                spec((STRETCH, vw), at),
                spec((4, qkv), fixed),
                spec((HALO, LANES), fixed),
                spec((1, DV), fixed),
            ],
            out_specs=[spec((STRETCH, width), at), spec((4, qkv), fixed), spec((HALO, LANES), fixed), spec((1, DV), fixed)],
            scratch_shapes=[pltpu.VMEM((heads, DK, DV), F32), pltpu.VMEM((STRETCH + HALO, qkv), F32)],
        ),
        out_shape=[
            jax.ShapeDtypeStruct((rows, width), LOW),
            jax.ShapeDtypeStruct((4, qkv), F32),
            jax.ShapeDtypeStruct((HALO, LANES), F32),
            jax.ShapeDtypeStruct((1, DV), F32),
        ],
        compiler_params=pltpu.CompilerParams(dimension_semantics=("arbitrary",), vmem_limit_bytes=32 << 20),
        cost_estimate=pl.CostEstimate(flops=1000, bytes_accessed=1000, transcendentals=0),
        name="mixer_backward",
    )(jnp.concatenate([keep, jnp.zeros((1,), jnp.int32)]), raw, conved, fresh, out, inv, start, grad, conv, rates, gain)


def product(left_rows, matrix):
    return lax.dot_general(left_rows, matrix, NN, preferred_element_type=F32)


def product_nt(left_rows, matrix):
    return lax.dot_general(left_rows, matrix, NT, preferred_element_type=F32)


def product_tn(left_rows, right_rows):
    return lax.dot_general(left_rows, right_rows, TN, preferred_element_type=F32)


def rms_rows(rows_in, gain_row):
    return (
        rows_in * lax.rsqrt(jnp.mean(rows_in * rows_in, axis=-1, keepdims=True) + 1e-06) * gain_row
    )


def layout(pack_lengths, pack_rows):
    positions = jnp.arange(pack_rows, dtype=jnp.int32)
    first_len = pack_lengths[0]
    second_len = pack_lengths[1]
    second_start = (first_len + STRETCH - 1) // STRETCH * STRETCH
    live_rows = (positions < first_len) | (positions >= second_start) & (
        positions < second_start + second_len
    )
    stretch_starts = jnp.arange(pack_rows // STRETCH, dtype=jnp.int32) * STRETCH
    keep_state = jnp.where(
        (stretch_starts == 0) | (stretch_starts == second_start), 0, 1
    ).astype(jnp.int32)
    return (keep_state, jnp.where(live_rows, 1.0, 0.0).astype(jnp.float32))


def rotation(count, shift):
    return [(i, (i + shift) % count) for i in range(count)]


def hold(*values):
    return lax.optimization_barrier(values)


def place_slots(found, axis):
    count = len(found)
    t = lax.axis_index("tensor")
    slots = []
    for slot in range(count):
        ahead = jnp.where(slot < t, slot - t + count, slot - t)
        chosen = found[0]
        for shift in range(1, count):
            chosen = jnp.where(ahead == shift, found[shift], chosen)
        slots.append(chosen)
    return jnp.concatenate(slots, axis=axis)


def z_fetch(own):
    count = lax.axis_size("tensor")
    return [own] + [
        lax.ppermute(own, "tensor", rotation(count, -shift)) for shift in range(1, count)
    ]


def queued_gather(own):
    return lax.all_gather(own, "tensor", axis=0, tiled=True)


def queued_scatter(partial):
    return lax.psum_scatter(
        partial.astype(jnp.bfloat16), "tensor", scatter_dimension=0, tiled=True
    )


def z_terms(partial):
    count = lax.axis_size("tensor")
    t = lax.axis_index("tensor")
    rows = partial.shape[0] // count
    parts = partial.reshape(count, rows, partial.shape[1])

    def take(ahead):
        index = jnp.where(t + ahead < count, t + ahead, t + ahead - count)
        return lax.dynamic_index_in_dim(parts, index, 0, keepdims=False)

    return take(0), [take(shift).astype(jnp.bfloat16) for shift in range(1, count)]


def z_ship(terms):
    count = lax.axis_size("tensor")
    return [
        lax.ppermute(term, "tensor", rotation(count, shift + 1)) for shift, term in enumerate(terms)
    ]


def z_sum(own, sent):
    for term in sent:
        own = own + term.astype(jnp.float32)
    return own


def relay_near(own):
    if lax.axis_size("tensor") != 4:
        return tuple(z_fetch(own))
    right = lax.ppermute(own, "tensor", [(0, 1), (1, 2), (2, 3)])
    left = lax.ppermute(own, "tensor", [(1, 0), (2, 1), (3, 2)])
    return own, right, left


def relay_far(near, axis):
    if lax.axis_size("tensor") != 4:
        return place_slots(near, axis)
    own, right, left = near
    t = lax.axis_index("tensor")
    right2 = lax.ppermute(right, "tensor", [(1, 2), (2, 3)])
    left2 = lax.ppermute(left, "tensor", [(1, 0), (2, 1)])
    far = lax.ppermute(jnp.where(t == 1, right, left), "tensor", [(1, 3), (2, 0)])

    def pick(a, b, c, d):
        return jnp.where(t == 0, a, jnp.where(t == 1, b, jnp.where(t == 2, c, d)))

    return jnp.concatenate(
        [
            pick(own, right, right2, far),
            pick(left, own, right, right2),
            pick(left2, left, own, right),
            pick(far, left2, left, own),
        ],
        axis=axis,
    )


def sum_over(values, axis):
    count = lax.axis_size(axis)
    if count & (count - 1):
        return lax.psum(values, axis)
    step = 1
    while step < count:
        values = values + lax.ppermute(values, axis, [(i, i ^ step) for i in range(count)])
        step *= 2
    return values


def gather_rows(local):
    return lax.all_gather(local, "dp", axis=0, tiled=True)


def scatter_rows(partial):
    return lax.psum_scatter(
        partial.astype(jnp.bfloat16), "dp", scatter_dimension=0, tiled=True
    ).astype(jnp.float32)


def shards(
    tokens,
    lengths,
    mixer_gain,
    query_weight,
    key_weight,
    value_weight,
    outgate_weight,
    alpha_weight,
    beta_weight,
    query_conv,
    key_conv,
    value_conv,
    log_rate,
    rate_bias,
    head_gain,
    output_weight,
    feed_gain,
    gate_weight,
    up_weight,
    down_weight,
    cotangent,
):
    tensor_index = lax.axis_index("tensor")
    tensor_count = lax.axis_size("tensor")
    micro_count, local_rows, width = tokens.shape
    pack_rows = local_rows * tensor_count
    key_width = query_weight.shape[1]
    value_width = value_weight.shape[1]
    head_count = alpha_weight.shape[1]
    hidden_width = gate_weight.shape[1]
    low = jnp.bfloat16

    edges = (key_width, 2 * key_width, 2 * key_width + value_width, 2 * key_width + 2 * value_width)
    pad = -(2 * head_count) % LANES
    in_local = jnp.concatenate(
        [
            query_weight,
            key_weight,
            value_weight,
            outgate_weight,
            alpha_weight,
            beta_weight,
            jnp.zeros((query_weight.shape[0], pad), low),
        ],
        axis=1,
    )
    in_full = gather_rows(in_local)
    out_full = gather_rows(output_weight.T)
    feed_full = gather_rows(jnp.concatenate([gate_weight, up_weight], axis=1))
    down_full = gather_rows(down_weight.T)

    small_local = (
        lax.dynamic_slice_in_dim(query_conv, tensor_index * key_width, key_width, 1),
        lax.dynamic_slice_in_dim(key_conv, tensor_index * key_width, key_width, 1),
        lax.dynamic_slice_in_dim(value_conv, tensor_index * value_width, value_width, 1),
        lax.dynamic_slice_in_dim(log_rate, tensor_index * head_count, head_count, 0),
        lax.dynamic_slice_in_dim(rate_bias, tensor_index * head_count, head_count, 0),
        head_gain,
    )
    packs = range(micro_count)
    wide = jnp.float32
    token_rows = [tokens[m].astype(wide) for m in packs]
    layouts = [layout(lengths[m, 0], pack_rows) for m in packs]
    own_masks = [
        lax.dynamic_slice_in_dim(row_mask, tensor_index * local_rows, local_rows, 0)[:, None]
        for _, row_mask in layouts
    ]
    out_grads = [cotangent[m].astype(wide) * own_masks[m] for m in packs]
    norm_ones = [jax.vjp(rms_rows, token_rows[m], mixer_gain) for m in packs]
    conv_local = jnp.concatenate(small_local[:3], axis=1)
    rates = jnp.zeros((HALO, LANES), wide)
    rates = rates.at[0, :head_count].set(small_local[3]).at[1, :head_count].set(small_local[4])
    gain_row = head_gain[None, :]
    joined = lambda *parts: jnp.concatenate(parts, axis=0)

    def mix(m, raw):
        mixed, *rest = mixer_forward(raw, layouts[m][0], conv_local, rates, gain_row, head_count)
        return mixed, rest

    def settle(m, received):
        middle = token_rows[m] + received.astype(wide)
        normed, back = jax.vjp(rms_rows, middle, feed_gain)
        return middle, normed.astype(low), back

    def feed_forward(second, hidden_grad):
        pre = product(second, feed_full)
        gate_pre, up_pre = pre[:, :hidden_width], pre[:, hidden_width:]
        gate_sig = jax.nn.sigmoid(gate_pre)
        gate_act = gate_pre * gate_sig
        hidden = (gate_act * up_pre).astype(low)
        gate_grad = hidden_grad * up_pre * gate_sig * (1.0 + gate_pre * (1.0 - gate_sig))
        feed_grad = jnp.concatenate([gate_grad, hidden_grad * gate_act], axis=1).astype(low)
        return hidden, feed_grad, product_nt(feed_grad, feed_full).astype(low)

    def feed_back(m, back, received):
        norm_grad, gain_grad = back(received.astype(wide))
        total = out_grads[m] + norm_grad
        return total, total.astype(low), gain_grad

    def mix_back(m, rows_in, raw, rest):
        return mixer_backward(
            raw, rest, product(rows_in, out_full), layouts[m][0], conv_local, rates, gain_row, head_count
        )

    A, B = 0, 1
    first_own = jnp.stack([norm_ones[m][0].astype(low) for m in packs])
    grad_own = jnp.stack([out_grads[m].astype(low) for m in packs])
    first_all = relay_far(relay_near(first_own), 1)
    first_all, in_full, grad_own = hold(first_all, in_full, grad_own)
    first_a, first_b = first_all[A], first_all[B]
    grad_near = relay_near(grad_own)
    raw_a = product(first_a, in_full)
    mixed_a, rest_a = mix(A, raw_a)
    mixed_a, *grad_near = hold(mixed_a, *grad_near)
    own_a, terms_a = z_terms(product_nt(mixed_a, out_full))
    sent_a = z_ship(terms_a)
    grad_all = relay_far(grad_near, 1)
    grad_a, grad_b = grad_all[A], grad_all[B]
    first_b, own_a = hold(first_b, own_a)
    raw_b = product(first_b, in_full)
    mixed_b, rest_b = mix(B, raw_b)
    mixed_b, own_a, feed_full, down_full, *sent_a = hold(
        mixed_b, own_a, feed_full, down_full, *sent_a
    )
    middle_a, normed_a, back_a = settle(A, z_sum(own_a, sent_a))
    second_a = queued_gather(normed_a)
    part_b = product_nt(mixed_b, out_full).astype(low)
    grad_a, grad_b, part_b = hold(grad_a, grad_b, part_b)
    hidden_grad_a = product(grad_a, down_full)
    hidden_grad_b = product(grad_b, down_full)
    second_a, part_b, hidden_grad_a, hidden_grad_b = hold(
        second_a, part_b, hidden_grad_a, hidden_grad_b
    )
    sum_b = queued_scatter(part_b)
    hidden_a, feed_grad_a, part2_a = feed_forward(second_a, hidden_grad_a)
    part2_a, sum_b = hold(part2_a, sum_b)
    sum2_a = queued_scatter(part2_a)
    middle_b, normed_b, back_b = settle(B, sum_b)
    result_a = z_terms(product_nt(hidden_a, down_full))
    normed_b, sum2_a, result_own = hold(normed_b, sum2_a, result_a[0])
    result_a = (result_own, result_a[1])
    second_b = queued_gather(normed_b)
    middle_grad_a, low_a, gain_grad_a = feed_back(A, back_a, sum2_a)
    low_a, second_b = hold(low_a, second_b)
    mix_rows_a = queued_gather(low_a)
    hidden_b, feed_grad_b, part2_b = feed_forward(second_b, hidden_grad_b)
    part2_b, mix_rows_a = hold(part2_b, mix_rows_a)
    sum2_b = queued_scatter(part2_b)
    result_b = z_terms(product_nt(hidden_b, down_full))
    feed_grad = product_tn(joined(second_a, second_b), joined(feed_grad_a, feed_grad_b)).astype(low)
    down_grad = product_tn(joined(grad_a, grad_b), joined(hidden_a, hidden_b)).astype(low)
    both_grad = jnp.concatenate([feed_grad, down_grad], axis=1)
    both_grad, sum2_b, mix_rows_a, result_own = hold(both_grad, sum2_b, mix_rows_a, result_b[0])
    result_b = (result_own, result_b[1])
    feed_width = 2 * hidden_width
    both_final = scatter_rows(both_grad)
    middle_grad_b, low_b, gain_grad_b = feed_back(B, back_b, sum2_b)
    mix_found_b = z_fetch(low_b)
    raw_grad_a, *core_a = mix_back(A, mix_rows_a, raw_a, rest_a)
    raw_grad_a, *mix_found_b = hold(raw_grad_a, *mix_found_b)
    mix_rows_b = place_slots(mix_found_b, 0)
    mix_rows_b, *final_terms = hold(mix_rows_b, *result_a[1])
    split_at = len(final_terms)
    final_a = (result_a[0], z_ship(final_terms))
    raw_grad_b, *core_b = mix_back(B, mix_rows_b, raw_b, rest_b)
    raw_grad_b, raw_grad_a, mixed_a, final_own, *sent_final = hold(
        raw_grad_b, raw_grad_a, mixed_a, final_a[0], *final_a[1]
    )
    final_a = (final_own, sent_final)
    raw_grad_b, *moved = hold(raw_grad_b, *result_b[1])
    final_b = (result_b[0], z_ship(moved))
    in_grad = product_tn(joined(first_a, first_b), joined(raw_grad_a, raw_grad_b)).astype(low)
    out_grad = product_tn(joined(mix_rows_a, mix_rows_b), joined(mixed_a, mixed_b)).astype(low)
    in_grad = jnp.concatenate([in_grad, out_grad], axis=1)
    raw_grad_a, in_grad, both_final, *moved = hold(raw_grad_a, in_grad, both_final, *final_b[1])
    final_b = (final_b[0], moved)
    part3_a = product_nt(raw_grad_a, in_full)
    own3_a, terms3_a = z_terms(part3_a)
    sent3_a = z_ship(terms3_a)
    last_final = scatter_rows(in_grad)
    in_final, out_final = last_final[:, : in_full.shape[1]], last_final[:, in_full.shape[1] :]
    part3_b = product_nt(raw_grad_b, in_full)
    own3_b, terms3_b = z_terms(part3_b)
    sent3_b = z_ship(terms3_b)
    outputs = [
        ((middle_a + z_sum(*final_a)) * own_masks[A]).astype(low),
        ((middle_b + z_sum(*final_b)) * own_masks[B]).astype(low),
    ]
    token_grad_a = norm_ones[A][1](z_sum(own3_a, sent3_a))[0]
    token_grad_b = norm_ones[B][1](z_sum(own3_b, sent3_b))[0]
    mixer_gain_grad = (
        jnp.sum(part3_a * first_a.astype(wide), axis=0)
        + jnp.sum(part3_b * first_b.astype(wide), axis=0)
    ) / mixer_gain
    input_grads = [middle_grad_a + token_grad_a, middle_grad_b + token_grad_b]
    feed_gain_grad = gain_grad_a + gain_grad_b
    conv_grads, rate_grads, gain_grads = [x + y for x, y in zip(core_a, core_b)]
    rate_grads, gain_grads = rate_grads[:2, :head_count], gain_grads[0]
    everywhere = jnp.concatenate([feed_gain_grad, mixer_gain_grad, gain_grads])
    per_slice = jnp.concatenate([conv_grads.reshape(-1), rate_grads.reshape(-1)])
    packed = sum_over(jnp.concatenate([per_slice, everywhere]), "dp")
    slices = jnp.zeros((tensor_count, per_slice.size), wide)
    slices = lax.dynamic_update_index_in_dim(slices, packed[: per_slice.size], tensor_index, 0)
    packed = sum_over(jnp.concatenate([slices.reshape(-1), packed[per_slice.size :]]), "tensor")
    slices = packed[: slices.size].reshape(tensor_count, per_slice.size)
    taps = query_conv.shape[0]
    conv_all = slices[:, : conv_grads.size].reshape(tensor_count, taps, -1)

    def all_columns(begin, end):
        return jnp.moveaxis(conv_all[:, :, begin:end], 0, 1).reshape(taps, -1)

    rate_all = slices[:, conv_grads.size :]
    everywhere = packed[slices.size :]
    return (
        jnp.stack(outputs),
        jnp.stack(input_grads),
        everywhere[width : 2 * width],
        in_final[:, : edges[0]],
        in_final[:, edges[0] : edges[1]],
        in_final[:, edges[1] : edges[2]],
        in_final[:, edges[2] : edges[3]],
        in_final[:, edges[3] : edges[3] + head_count],
        in_final[:, edges[3] + head_count : edges[3] + 2 * head_count],
        all_columns(0, edges[0]),
        all_columns(edges[0], edges[1]),
        all_columns(edges[1], edges[2]),
        rate_all[:, :head_count].reshape(-1),
        rate_all[:, head_count:].reshape(-1),
        everywhere[2 * width :],
        out_final.T,
        everywhere[:width],
        both_final[:, :hidden_width],
        both_final[:, hidden_width:feed_width],
        both_final[:, feed_width:].T,
    )


def solution(mesh):
    return jax.shard_map(
        shards,
        mesh=mesh,
        in_specs=(
            P(None, ("dp", "tensor"), None),
            P(None, "dp", None),
            P(),
            P("dp", "tensor"),
            P("dp", "tensor"),
            P("dp", "tensor"),
            P("dp", "tensor"),
            P("dp", "tensor"),
            P("dp", "tensor"),
            P(),
            P(),
            P(),
            P(),
            P(),
            P(),
            P("tensor", "dp"),
            P(),
            P("dp", "tensor"),
            P("dp", "tensor"),
            P("tensor", "dp"),
            P(None, ("dp", "tensor"), None),
        ),
        out_specs=(
            P(None, ("dp", "tensor"), None),
            P(None, ("dp", "tensor"), None),
            P(),
            P("dp", "tensor"),
            P("dp", "tensor"),
            P("dp", "tensor"),
            P("dp", "tensor"),
            P("dp", "tensor"),
            P("dp", "tensor"),
            P(),
            P(),
            P(),
            P(),
            P(),
            P(),
            P("tensor", "dp"),
            P(),
            P("dp", "tensor"),
            P("dp", "tensor"),
            P("tensor", "dp"),
        ),
        check_vma=False,
    )
```

```python
import functools
import jax
import jax.numpy as jnp
from jax import lax
from jax.experimental import pallas as pl
from jax.experimental.pallas import tpu as pltpu
from jax.sharding import PartitionSpec as P

DK = 128
DV = 256
STRETCH = 64
LANES = 128
HALO = 8
F32 = jnp.float32
LOW = jnp.bfloat16

NN = (((1,), (0,)), ((), ()))
NT = (((1,), (1,)), ((), ()))
TN = (((0,), (0,)), ((), ()))


def split(a):
    hi = a.astype(LOW)
    return hi, (a - hi.astype(F32)).astype(LOW)


def mm(a, b, dims=NN, passes=1):
    if passes == 6:
        return lax.dot_general(a, b, dims, precision=lax.Precision.HIGHEST, preferred_element_type=F32)
    dot = functools.partial(lax.dot_general, dimension_numbers=dims, preferred_element_type=F32)
    if passes == 1:
        return dot(a.astype(LOW), b.astype(LOW))
    ah, al = split(a)
    bh, bl = split(b)
    return dot(ah, bh) + (dot(ah, bl) + dot(al, bh))


def block_masks():
    row = lax.broadcasted_iota(jnp.int32, (STRETCH, STRETCH), 0)
    col = lax.broadcasted_iota(jnp.int32, (STRETCH, STRETCH), 1)
    return row, col


def sigmoid(v):
    return 1.0 / (1.0 + jnp.exp(-v))


def softplus(v):
    return jnp.maximum(v, 0.0) + jnp.log1p(jnp.exp(-jnp.abs(v)))


def unit_inverses(lowers, passes):
    row, col = block_masks()
    eye = jnp.where(row == col, 1.0, 0.0)
    pair = (row // 2 == col // 2) & (row > col)
    inverses = [eye - jnp.where(pair, lower, 0.0) for lower in lowers]
    size = 2
    while size < STRETCH:
        off = (row // (2 * size) == col // (2 * size)) & (row // size > col // size)
        offs = [jnp.where(off, lower, 0.0) for lower in lowers]
        halves = [mm(inv, o, NN, passes) for inv, o in zip(inverses, offs)]
        inverses = [inv - mm(h, inv, NN, passes) for inv, h in zip(inverses, halves)]
        size *= 2
    return inverses


def decay_parts(mixed, rates, heads):
    lane = lax.broadcasted_iota(jnp.int32, (STRETCH, LANES), 1)
    row, col = block_masks()
    soft_in = mixed + rates[1:2, :]
    decay = jnp.where(lane < heads, -jnp.exp(rates[0:1, :]) * softplus(soft_in), 0.0)
    tri = jnp.where(row >= col, 1.0, 0.0)
    upper = jnp.where(row <= col, 1.0, 0.0)
    sum_col = mm(tri, decay, NN, 6)
    sum_row = mm(decay[:, :HALO], upper, TN, 6)
    return decay, soft_in, sum_col, sum_row


def forward_kernel(heads, keep_ref, raw_ref, conv_ref, rates_ref, gain_ref,
                   gated_ref, conved_ref, fresh_ref, out_ref, inv_ref, start_ref, state, ext):
    n = pl.program_id(0)
    keep = keep_ref[n].astype(F32)
    kw, vw = heads * DK, heads * DV
    qkv = 2 * kw + vw
    span = STRETCH

    @pl.when(n == 0)
    def _():
        state[...] = jnp.zeros_like(state)
        ext[...] = jnp.zeros_like(ext)

    ext[0:HALO, :] = ext[span:span + HALO, :] * keep
    ext[HALO:HALO + span, :] = raw_ref[:, :qkv]

    def conv(begin, width):
        total = ext[HALO:HALO + span, begin:begin + width] * conv_ref[0:1, begin:begin + width]
        for j in range(1, 4):
            total = total + ext[HALO - j:HALO - j + span, begin:begin + width] * conv_ref[j:j + 1, begin:begin + width]
        conved_ref[:, begin:begin + width] = total
        return total * sigmoid(total)

    mixed = raw_ref[:, qkv + vw:]
    decay, _, sum_col, sum_row = decay_parts(mixed, rates_ref[...], heads)
    beta_all = sigmoid(mixed)
    row, col = block_masks()
    incl, strict = row >= col, row > col
    qs, ks, lowers, scores, betas = [], [], [], [], []
    for h in range(heads):
        zq = conv(h * DK, DK)
        zk = conv(kw + h * DK, DK)
        q = zq * lax.rsqrt(jnp.sum(zq * zq, axis=-1, keepdims=True) + 1e-6) * DK ** -0.5
        k = zk * lax.rsqrt(jnp.sum(zk * zk, axis=-1, keepdims=True) + 1e-6)
        within = jnp.exp(jnp.where(incl, sum_col[:, h:h + 1] - sum_row[h:h + 1, :], -1e30))
        beta = beta_all[:, heads + h:heads + h + 1]
        scores.append(mm(q, k, NT, 3) * within)
        lowers.append(jnp.where(strict, beta * mm(k, k, NT, 3) * within, 0.0))
        qs.append(q); ks.append(k); betas.append(beta)
    inverses = unit_inverses(lowers, 3)
    for h in range(heads):
        q, k, beta = qs[h], ks[h], betas[h]
        start = state[h] * keep
        total = sum_col[:, h:h + 1]
        growth = jnp.exp(total)
        last = total[span - 1:span, :]
        v = conv(2 * kw + h * DV, DV)
        k_state = mm(k, start, NN, 3)
        q_state = mm(q, start, NN, 3)
        fresh = mm(inverses[h], beta * (v - growth * k_state), NN, 3)
        out = growth * q_state + mm(scores[h], fresh, NN, 3)
        tail = jnp.exp(last - total)
        state[h] = jnp.exp(last) * start + mm(k * tail, fresh, TN, 3)
        cols = slice(h * DV, (h + 1) * DV)
        fresh_ref[:, cols] = fresh.astype(fresh_ref.dtype)
        out_ref[:, cols] = out
        inv_ref[0, h] = inverses[h].astype(inv_ref.dtype)
        start_ref[0, h] = start.astype(start_ref.dtype)
        gate = raw_ref[:, qkv + h * DV:qkv + (h + 1) * DV]
        normed = out * lax.rsqrt(jnp.mean(out * out, axis=-1, keepdims=True) + 1e-5) * gain_ref[...]
        gated_ref[:, cols] = (normed * (gate * sigmoid(gate))).astype(LOW)


def mixer_forward(raw, keep, conv, rates, gain, heads):
    rows, width = raw.shape
    count = rows // STRETCH
    kw, vw = heads * DK, heads * DV
    qkv = 2 * kw + vw
    at = lambda n, keep_ref: (n, 0)
    fixed = lambda n, keep_ref: (0, 0)
    at4 = lambda n, keep_ref: (n, 0, 0, 0)
    spec = pl.BlockSpec
    return pl.pallas_call(
        functools.partial(forward_kernel, heads),
        grid_spec=pltpu.PrefetchScalarGridSpec(
            num_scalar_prefetch=1,
            grid=(count,),
            in_specs=[spec((STRETCH, width), at), spec((4, qkv), fixed), spec((HALO, LANES), fixed), spec((1, DV), fixed)],
            out_specs=[
                spec((STRETCH, vw), at),
                spec((STRETCH, qkv), at),
                spec((STRETCH, vw), at),
                spec((STRETCH, vw), at),
                spec((1, heads, STRETCH, STRETCH), at4),
                spec((1, heads, DK, DV), at4),
            ],
            scratch_shapes=[pltpu.VMEM((heads, DK, DV), F32), pltpu.VMEM((STRETCH + HALO, qkv), F32)],
        ),
        out_shape=[
            jax.ShapeDtypeStruct((rows, vw), LOW),
            jax.ShapeDtypeStruct((rows, qkv), F32),
            jax.ShapeDtypeStruct((rows, vw), F32),
            jax.ShapeDtypeStruct((rows, vw), F32),
            jax.ShapeDtypeStruct((count, heads, STRETCH, STRETCH), F32),
            jax.ShapeDtypeStruct((count, heads, DK, DV), F32),
        ],
        compiler_params=pltpu.CompilerParams(dimension_semantics=("arbitrary",), vmem_limit_bytes=32 << 20),
        cost_estimate=pl.CostEstimate(flops=1000, bytes_accessed=1000, transcendentals=0),
        name="mixer_forward",
    )(keep, raw, conv, rates, gain)


def backward_kernel(heads, keep_ref, raw_ref, conved_ref, fresh_ref, out_ref, inv_ref, start_ref, grad_ref,
                    conv_ref, rates_ref, gain_ref,
                    draw_ref, dconv_ref, drates_ref, dgain_ref, dstate, ext):
    i = pl.program_id(0)
    count = pl.num_programs(0)
    n = count - 1 - i
    keep_next = keep_ref[n + 1].astype(F32)
    kw, vw = heads * DK, heads * DV
    qkv = 2 * kw + vw
    span = STRETCH

    @pl.when(i == 0)
    def _():
        dstate[...] = jnp.zeros_like(dstate)
        ext[...] = jnp.zeros_like(ext)
        dconv_ref[...] = jnp.zeros_like(dconv_ref)
        drates_ref[...] = jnp.zeros_like(drates_ref)
        dgain_ref[...] = jnp.zeros_like(dgain_ref)

    ext[span:span + HALO, :] = ext[0:HALO, :] * keep_next
    rates = rates_ref[...]
    mixed = raw_ref[:, qkv + vw:]
    decay, soft_in, sum_col, sum_row = decay_parts(mixed, rates, heads)
    beta_all = sigmoid(mixed)
    row, col = block_masks()
    incl, strict = row >= col, row > col
    lane = lax.broadcasted_iota(jnp.int32, (span, LANES), 1)
    last_row = lax.broadcasted_iota(jnp.int32, (span, 1), 0) == span - 1
    gain = gain_ref[...]
    dgain = jnp.zeros((1, DV), F32)
    dsum_all = jnp.zeros((span, LANES), F32)
    dbeta_all = jnp.zeros((span, LANES), F32)
    down_rows = []

    def act(begin, width):
        c = conved_ref[:, begin:begin + width]
        s = sigmoid(c)
        return c * s, s * (1.0 + c * (1.0 - s))

    for h in range(heads):
        cols = slice(h * DV, (h + 1) * DV)
        zq, slope_q = act(h * DK, DK)
        zk, slope_k = act(kw + h * DK, DK)
        v, slope_v = act(2 * kw + h * DV, DV)
        rq = lax.rsqrt(jnp.sum(zq * zq, axis=-1, keepdims=True) + 1e-6)
        rk = lax.rsqrt(jnp.sum(zk * zk, axis=-1, keepdims=True) + 1e-6)
        q = zq * rq * DK ** -0.5
        k = zk * rk
        within = jnp.exp(jnp.where(incl, sum_col[:, h:h + 1] - sum_row[h:h + 1, :], -1e30))
        beta = beta_all[:, heads + h:heads + h + 1]
        total = sum_col[:, h:h + 1]
        growth = jnp.exp(total)
        last = total[span - 1:span, :]
        growth_last = jnp.exp(last)
        tail = jnp.exp(last - total)
        start = start_ref[0, h].astype(F32)
        fresh = fresh_ref[:, cols].astype(F32)
        inv = inv_ref[0, h]
        scores = mm(q, k, NT, 3) * within
        inner = mm(k, k, NT, 3)
        k_state = mm(k, start, NN, 3)
        q_state = mm(q, start, NN, 3)
        out = out_ref[:, cols]
        gate = raw_ref[:, qkv + h * DV:qkv + (h + 1) * DV]
        gate_sig = sigmoid(gate)
        gate_act = gate * gate_sig
        dgated = grad_ref[:, cols].astype(F32)
        r = lax.rsqrt(jnp.mean(out * out, axis=-1, keepdims=True) + 1e-5)
        unit = out * r
        dnormed = dgated * gate_act
        draw_ref[:, qkv + h * DV:qkv + (h + 1) * DV] = (
            dgated * (unit * gain) * (gate_sig * (1.0 + gate * (1.0 - gate_sig)))
        ).astype(LOW)
        dgain = dgain + jnp.sum(dnormed * unit, axis=0, keepdims=True)
        dunit = dnormed * gain
        dout = r * (dunit - unit * jnp.mean(dunit * unit, axis=-1, keepdims=True))
        dnext = dstate[h] * keep_next
        dfresh = mm(scores, dout, TN, 1) + mm(k * tail, dnext, NN, 1)
        dright = mm(inv, dfresh, TN, 1)
        dscores = jnp.where(incl, mm(dout, fresh, NT, 1), 0.0)
        dlower = jnp.where(strict, -mm(dright, fresh, NT, 1), 0.0)
        scaled = beta * growth * dright
        dstate[h] = growth_last * dnext + mm(q * growth, dout, TN, 1) - mm(k, scaled, TN, 1)
        dv = beta * dright
        dbeta = jnp.sum(dright * (v - growth * k_state), axis=-1, keepdims=True)
        dgrowth = jnp.sum(dout * q_state - dv * k_state, axis=-1, keepdims=True)
        dsw = dscores * within
        dq = growth * mm(dout, start, NT, 1) + mm(dsw, k, NN, 1)
        into_k = mm(fresh, dnext, NT, 1)
        dinner = dlower * within
        dbeta = dbeta + jnp.sum(dinner * inner, axis=-1, keepdims=True)
        weighted = beta * dinner
        dk = (
            tail * into_k
            - mm(scaled, start, NT, 1)
            + mm(dsw, q, TN, 1)
            + mm(weighted, k, NN, 1)
            + mm(weighted, k, TN, 1)
        )
        tailed = tail * jnp.sum(k * into_k, axis=-1, keepdims=True)
        pairs = dscores * scores + weighted * inner
        at_last = growth_last * jnp.sum(start * dnext, keepdims=True) + jnp.sum(tailed, keepdims=True)
        dsum = jnp.sum(pairs, axis=-1, keepdims=True) + growth * dgrowth - tailed + jnp.where(last_row, at_last, 0.0)
        down_rows.append(jnp.sum(pairs, axis=0, keepdims=True))
        dsum_all = jnp.where(lane == h, dsum, dsum_all)
        dbeta_all = jnp.where(lane == heads + h, dbeta, dbeta_all)
        dzq = (DK ** -0.5 * rq) * (dq - zq * (rq * rq * jnp.sum(dq * zq, axis=-1, keepdims=True)))
        dzk = rk * (dk - zk * (rk * rk * jnp.sum(dk * zk, axis=-1, keepdims=True)))
        ext[0:span, h * DK:(h + 1) * DK] = dzq * slope_q
        ext[0:span, kw + h * DK:kw + (h + 1) * DK] = dzk * slope_k
        ext[0:span, 2 * kw + h * DV:2 * kw + (h + 1) * DV] = dv * slope_v

    dgain_ref[...] += dgain
    upper = jnp.where(row <= col, 1.0, 0.0)
    down = jnp.concatenate(down_rows + [jnp.zeros((LANES - heads, span), F32)], axis=0)
    ddecay = mm(upper, dsum_all, NN, 6) - mm(upper, down, NT, 6)
    ddecay = jnp.where(lane < heads, ddecay, 0.0)
    dalpha = ddecay * (-jnp.exp(rates[0:1, :])) * sigmoid(soft_in)
    dbeta_raw = jnp.where((lane >= heads) & (lane < 2 * heads), dbeta_all * beta_all * (1.0 - beta_all), 0.0)
    draw_ref[:, qkv + vw:] = (dalpha + dbeta_raw).astype(LOW)
    drates_ref[0:1, :] += jnp.sum(ddecay * decay, axis=0, keepdims=True)
    drates_ref[1:2, :] += jnp.sum(dalpha, axis=0, keepdims=True)
    wide = 256
    for begin in range(0, qkv, wide):
        cols = slice(begin, begin + wide)
        raw = raw_ref[:, cols]
        total = None
        for j in range(4):
            shifted = ext[j:j + span, cols]
            term = shifted * conv_ref[j:j + 1, cols]
            total = term if total is None else total + term
            dconv_ref[j:j + 1, cols] += jnp.sum(raw * shifted, axis=0, keepdims=True)
        draw_ref[:, cols] = total.astype(LOW)


def mixer_backward(raw, kept, grad, keep, conv, rates, gain, heads):
    conved, fresh, out, inv, start = kept
    rows, width = raw.shape
    count = rows // STRETCH
    kw, vw = heads * DK, heads * DV
    qkv = 2 * kw + vw
    at = lambda i, keep_ref: (count - 1 - i, 0)
    fixed = lambda i, keep_ref: (0, 0)
    at4 = lambda i, keep_ref: (count - 1 - i, 0, 0, 0)
    spec = pl.BlockSpec
    return pl.pallas_call(
        functools.partial(backward_kernel, heads),
        grid_spec=pltpu.PrefetchScalarGridSpec(
            num_scalar_prefetch=1,
            grid=(count,),
            in_specs=[
                spec((STRETCH, width), at),
                spec((STRETCH, qkv), at),
                spec((STRETCH, vw), at),
                spec((STRETCH, vw), at),
                spec((1, heads, STRETCH, STRETCH), at4),
                spec((1, heads, DK, DV), at4),
                spec((STRETCH, vw), at),
                spec((4, qkv), fixed),
                spec((HALO, LANES), fixed),
                spec((1, DV), fixed),
            ],
            out_specs=[spec((STRETCH, width), at), spec((4, qkv), fixed), spec((HALO, LANES), fixed), spec((1, DV), fixed)],
            scratch_shapes=[pltpu.VMEM((heads, DK, DV), F32), pltpu.VMEM((STRETCH + HALO, qkv), F32)],
        ),
        out_shape=[
            jax.ShapeDtypeStruct((rows, width), LOW),
            jax.ShapeDtypeStruct((4, qkv), F32),
            jax.ShapeDtypeStruct((HALO, LANES), F32),
            jax.ShapeDtypeStruct((1, DV), F32),
        ],
        compiler_params=pltpu.CompilerParams(dimension_semantics=("arbitrary",), vmem_limit_bytes=32 << 20),
        cost_estimate=pl.CostEstimate(flops=1000, bytes_accessed=1000, transcendentals=0),
        name="mixer_backward",
    )(jnp.concatenate([keep, jnp.zeros((1,), jnp.int32)]), raw, conved, fresh, out, inv, start, grad, conv, rates, gain)


def product(left_rows, matrix):
    return lax.dot_general(left_rows, matrix, NN, preferred_element_type=F32)


def product_nt(left_rows, matrix):
    return lax.dot_general(left_rows, matrix, NT, preferred_element_type=F32)


def product_tn(left_rows, right_rows):
    return lax.dot_general(left_rows, right_rows, TN, preferred_element_type=F32)


def rms_rows(rows_in, gain_row):
    return (
        rows_in * lax.rsqrt(jnp.mean(rows_in * rows_in, axis=-1, keepdims=True) + 1e-06) * gain_row
    )


def layout(pack_lengths, pack_rows):
    positions = jnp.arange(pack_rows, dtype=jnp.int32)
    first_len = pack_lengths[0]
    second_len = pack_lengths[1]
    second_start = (first_len + STRETCH - 1) // STRETCH * STRETCH
    live_rows = (positions < first_len) | (positions >= second_start) & (
        positions < second_start + second_len
    )
    stretch_starts = jnp.arange(pack_rows // STRETCH, dtype=jnp.int32) * STRETCH
    keep_state = jnp.where(
        (stretch_starts == 0) | (stretch_starts == second_start), 0, 1
    ).astype(jnp.int32)
    return (keep_state, jnp.where(live_rows, 1.0, 0.0).astype(jnp.float32))


def rotation(count, shift):
    return [(i, (i + shift) % count) for i in range(count)]


def hold(*values):
    return lax.optimization_barrier(values)


def place_slots(found, axis):
    count = len(found)
    t = lax.axis_index("tensor")
    slots = []
    for slot in range(count):
        ahead = jnp.where(slot < t, slot - t + count, slot - t)
        chosen = found[0]
        for shift in range(1, count):
            chosen = jnp.where(ahead == shift, found[shift], chosen)
        slots.append(chosen)
    return jnp.concatenate(slots, axis=axis)


def z_fetch(own):
    count = lax.axis_size("tensor")
    return [own] + [
        lax.ppermute(own, "tensor", rotation(count, -shift)) for shift in range(1, count)
    ]


def queued_gather(own):
    return lax.all_gather(own, "tensor", axis=0, tiled=True)


def queued_scatter(partial):
    return lax.psum_scatter(
        partial.astype(jnp.bfloat16), "tensor", scatter_dimension=0, tiled=True
    )


def z_terms(partial):
    count = lax.axis_size("tensor")
    t = lax.axis_index("tensor")
    rows = partial.shape[0] // count
    parts = partial.reshape(count, rows, partial.shape[1])

    def take(ahead):
        index = jnp.where(t + ahead < count, t + ahead, t + ahead - count)
        return lax.dynamic_index_in_dim(parts, index, 0, keepdims=False)

    return take(0), [take(shift).astype(jnp.bfloat16) for shift in range(1, count)]


def z_ship(terms):
    count = lax.axis_size("tensor")
    return [
        lax.ppermute(term, "tensor", rotation(count, shift + 1)) for shift, term in enumerate(terms)
    ]


def z_sum(own, sent):
    for term in sent:
        own = own + term.astype(jnp.float32)
    return own


def relay_near(own):
    if lax.axis_size("tensor") != 4:
        return tuple(z_fetch(own))
    right = lax.ppermute(own, "tensor", [(0, 1), (1, 2), (2, 3)])
    left = lax.ppermute(own, "tensor", [(1, 0), (2, 1), (3, 2)])
    return own, right, left


def relay_far(near, axis):
    if lax.axis_size("tensor") != 4:
        return place_slots(near, axis)
    own, right, left = near
    t = lax.axis_index("tensor")
    right2 = lax.ppermute(right, "tensor", [(1, 2), (2, 3)])
    left2 = lax.ppermute(left, "tensor", [(1, 0), (2, 1)])
    far = lax.ppermute(jnp.where(t == 1, right, left), "tensor", [(1, 3), (2, 0)])

    def pick(a, b, c, d):
        return jnp.where(t == 0, a, jnp.where(t == 1, b, jnp.where(t == 2, c, d)))

    return jnp.concatenate(
        [
            pick(own, right, right2, far),
            pick(left, own, right, right2),
            pick(left2, left, own, right),
            pick(far, left2, left, own),
        ],
        axis=axis,
    )


def sum_over(values, axis):
    count = lax.axis_size(axis)
    if count & (count - 1):
        return lax.psum(values, axis)
    step = 1
    while step < count:
        values = values + lax.ppermute(values, axis, [(i, i ^ step) for i in range(count)])
        step *= 2
    return values


def gather_rows(local):
    return lax.all_gather(local, "dp", axis=0, tiled=True)


def scatter_rows(partial):
    return lax.psum_scatter(
        partial.astype(jnp.bfloat16), "dp", scatter_dimension=0, tiled=True
    ).astype(jnp.float32)


def relay_scatter(partial):
    count = lax.axis_size("tensor")
    packs, rows, width = partial.shape
    low, wide = jnp.bfloat16, jnp.float32
    if count != 4:
        return lax.psum_scatter(
            partial.astype(low), "tensor", scatter_dimension=1, tiled=True
        ).astype(wide)
    t = lax.axis_index("tensor")
    parts = partial.reshape(packs, count, rows // count, width)

    def take(index):
        return lax.dynamic_index_in_dim(parts, jnp.clip(index, 0, count - 1), 1, keepdims=False)

    far = lax.ppermute(
        take(jnp.where(t == 3, 0, 3)).astype(low), "tensor", [(3, 1), (0, 2)]
    )
    left = lax.ppermute(take(t - 2).astype(low), "tensor", [(3, 2), (2, 1)])
    right = lax.ppermute(take(t + 2).astype(low), "tensor", [(0, 1), (1, 2)])
    to_left = take(t - 1) + left.astype(wide) + jnp.where(t == 1, far, 0).astype(wide)
    to_right = take(t + 1) + right.astype(wide) + jnp.where(t == 2, far, 0).astype(wide)
    from_right = lax.ppermute(to_left.astype(low), "tensor", [(1, 0), (2, 1), (3, 2)])
    from_left = lax.ppermute(to_right.astype(low), "tensor", [(0, 1), (1, 2), (2, 3)])
    return take(t) + from_right.astype(wide) + from_left.astype(wide)


def shards(
    tokens,
    lengths,
    mixer_gain,
    query_weight,
    key_weight,
    value_weight,
    outgate_weight,
    alpha_weight,
    beta_weight,
    query_conv,
    key_conv,
    value_conv,
    log_rate,
    rate_bias,
    head_gain,
    output_weight,
    feed_gain,
    gate_weight,
    up_weight,
    down_weight,
    cotangent,
):
    tensor_index = lax.axis_index("tensor")
    tensor_count = lax.axis_size("tensor")
    micro_count, local_rows, width = tokens.shape
    pack_rows = local_rows * tensor_count
    key_width = query_weight.shape[1]
    value_width = value_weight.shape[1]
    head_count = alpha_weight.shape[1]
    hidden_width = gate_weight.shape[1]
    low = jnp.bfloat16

    edges = (key_width, 2 * key_width, 2 * key_width + value_width, 2 * key_width + 2 * value_width)
    pad = -(2 * head_count) % LANES
    in_local = jnp.concatenate(
        [
            query_weight,
            key_weight,
            value_weight,
            outgate_weight,
            alpha_weight,
            beta_weight,
            jnp.zeros((query_weight.shape[0], pad), low),
        ],
        axis=1,
    )
    in_full = gather_rows(in_local)
    out_full = gather_rows(output_weight.T)
    feed_full = gather_rows(jnp.concatenate([gate_weight, up_weight], axis=1))
    down_full = gather_rows(down_weight.T)

    small_local = (
        lax.dynamic_slice_in_dim(query_conv, tensor_index * key_width, key_width, 1),
        lax.dynamic_slice_in_dim(key_conv, tensor_index * key_width, key_width, 1),
        lax.dynamic_slice_in_dim(value_conv, tensor_index * value_width, value_width, 1),
        lax.dynamic_slice_in_dim(log_rate, tensor_index * head_count, head_count, 0),
        lax.dynamic_slice_in_dim(rate_bias, tensor_index * head_count, head_count, 0),
        head_gain,
    )
    packs = range(micro_count)
    wide = jnp.float32
    token_rows = [tokens[m].astype(wide) for m in packs]
    layouts = [layout(lengths[m, 0], pack_rows) for m in packs]
    own_masks = [
        lax.dynamic_slice_in_dim(row_mask, tensor_index * local_rows, local_rows, 0)[:, None]
        for _, row_mask in layouts
    ]
    out_grads = [cotangent[m].astype(wide) * own_masks[m] for m in packs]
    norm_ones = [jax.vjp(rms_rows, token_rows[m], mixer_gain) for m in packs]
    conv_local = jnp.concatenate(small_local[:3], axis=1)
    rates = jnp.zeros((HALO, LANES), wide)
    rates = rates.at[0, :head_count].set(small_local[3]).at[1, :head_count].set(small_local[4])
    gain_row = head_gain[None, :]
    joined = lambda *parts: jnp.concatenate(parts, axis=0)

    def mix(m, raw):
        mixed, *rest = mixer_forward(raw, layouts[m][0], conv_local, rates, gain_row, head_count)
        return mixed, rest

    def settle(m, received):
        middle = token_rows[m] + received.astype(wide)
        normed, back = jax.vjp(rms_rows, middle, feed_gain)
        return middle, normed.astype(low), back

    def feed_forward(second, hidden_grad):
        pre = product(second, feed_full)
        gate_pre, up_pre = pre[:, :hidden_width], pre[:, hidden_width:]
        gate_sig = jax.nn.sigmoid(gate_pre)
        gate_act = gate_pre * gate_sig
        hidden = (gate_act * up_pre).astype(low)
        gate_grad = hidden_grad * up_pre * gate_sig * (1.0 + gate_pre * (1.0 - gate_sig))
        feed_grad = jnp.concatenate([gate_grad, hidden_grad * gate_act], axis=1).astype(low)
        return hidden, feed_grad, product_nt(feed_grad, feed_full).astype(low)

    def feed_back(m, back, received):
        norm_grad, gain_grad = back(received.astype(wide))
        total = out_grads[m] + norm_grad
        return total, total.astype(low), gain_grad

    def mix_back(m, rows_in, raw, rest):
        return mixer_backward(
            raw, rest, product(rows_in, out_full), layouts[m][0], conv_local, rates, gain_row, head_count
        )

    A, B = 0, 1
    first_own = jnp.stack([norm_ones[m][0].astype(low) for m in packs])
    grad_own = jnp.stack([out_grads[m].astype(low) for m in packs])
    first_all = relay_far(relay_near(first_own), 1)
    first_all, in_full, grad_own = hold(first_all, in_full, grad_own)
    first_a, first_b = first_all[A], first_all[B]
    grad_near = relay_near(grad_own)
    raw_a = product(first_a, in_full)
    mixed_a, rest_a = mix(A, raw_a)
    mixed_a, *grad_near = hold(mixed_a, *grad_near)
    own_a, terms_a = z_terms(product_nt(mixed_a, out_full))
    sent_a = z_ship(terms_a)
    grad_all = relay_far(grad_near, 1)
    grad_a, grad_b = grad_all[A], grad_all[B]
    first_b, own_a = hold(first_b, own_a)
    raw_b = product(first_b, in_full)
    mixed_b, rest_b = mix(B, raw_b)
    mixed_b, own_a, feed_full, down_full, *sent_a = hold(
        mixed_b, own_a, feed_full, down_full, *sent_a
    )
    middle_a, normed_a, back_a = settle(A, z_sum(own_a, sent_a))
    second_a = queued_gather(normed_a)
    part_b = product_nt(mixed_b, out_full).astype(low)
    grad_a, grad_b, part_b = hold(grad_a, grad_b, part_b)
    hidden_grad_a = product(grad_a, down_full)
    hidden_grad_b = product(grad_b, down_full)
    second_a, part_b, hidden_grad_a, hidden_grad_b = hold(
        second_a, part_b, hidden_grad_a, hidden_grad_b
    )
    sum_b = queued_scatter(part_b)
    hidden_a, feed_grad_a, part2_a = feed_forward(second_a, hidden_grad_a)
    part2_a, sum_b = hold(part2_a, sum_b)
    sum2_a = queued_scatter(part2_a)
    middle_b, normed_b, back_b = settle(B, sum_b)
    result_a = z_terms(product_nt(hidden_a, down_full))
    normed_b, sum2_a, result_own = hold(normed_b, sum2_a, result_a[0])
    result_a = (result_own, result_a[1])
    second_b = queued_gather(normed_b)
    middle_grad_a, low_a, gain_grad_a = feed_back(A, back_a, sum2_a)
    low_a, second_b = hold(low_a, second_b)
    mix_rows_a = queued_gather(low_a)
    hidden_b, feed_grad_b, part2_b = feed_forward(second_b, hidden_grad_b)
    part2_b, mix_rows_a = hold(part2_b, mix_rows_a)
    sum2_b = queued_scatter(part2_b)
    result_b = z_terms(product_nt(hidden_b, down_full))
    feed_grad = product_tn(joined(second_a, second_b), joined(feed_grad_a, feed_grad_b)).astype(low)
    down_grad = product_tn(joined(grad_a, grad_b), joined(hidden_a, hidden_b)).astype(low)
    both_grad = jnp.concatenate([feed_grad, down_grad], axis=1)
    both_grad, sum2_b, mix_rows_a, result_own = hold(both_grad, sum2_b, mix_rows_a, result_b[0])
    result_b = (result_own, result_b[1])
    feed_width = 2 * hidden_width
    both_final = scatter_rows(both_grad)
    middle_grad_b, low_b, gain_grad_b = feed_back(B, back_b, sum2_b)
    mix_found_b = z_fetch(low_b)
    raw_grad_a, *core_a = mix_back(A, mix_rows_a, raw_a, rest_a)
    raw_grad_a, *mix_found_b = hold(raw_grad_a, *mix_found_b)
    mix_rows_b = place_slots(mix_found_b, 0)
    mix_rows_b, *final_terms = hold(mix_rows_b, *result_a[1])
    split_at = len(final_terms)
    final_a = (result_a[0], z_ship(final_terms))
    raw_grad_b, *core_b = mix_back(B, mix_rows_b, raw_b, rest_b)
    raw_grad_b, raw_grad_a, mixed_a, final_own, *sent_final = hold(
        raw_grad_b, raw_grad_a, mixed_a, final_a[0], *final_a[1]
    )
    final_a = (final_own, sent_final)
    raw_grad_b, *moved = hold(raw_grad_b, *result_b[1])
    final_b = (result_b[0], z_ship(moved))
    in_grad = product_tn(joined(first_a, first_b), joined(raw_grad_a, raw_grad_b)).astype(low)
    out_grad = product_tn(joined(mix_rows_a, mix_rows_b), joined(mixed_a, mixed_b)).astype(low)
    in_grad = jnp.concatenate([in_grad, out_grad], axis=1)
    raw_grad_a, in_grad, both_final, *moved = hold(raw_grad_a, in_grad, both_final, *final_b[1])
    final_b = (final_b[0], moved)
    part3_a = product_nt(raw_grad_a, in_full)
    last_final = scatter_rows(in_grad)
    in_final, out_final = last_final[:, : in_full.shape[1]], last_final[:, in_full.shape[1] :]
    part3_b = product_nt(raw_grad_b, in_full)
    first_sum = [relay_scatter(part3_a[None])[0], relay_scatter(part3_b[None])[0]]
    outputs = [
        ((middle_a + z_sum(*final_a)) * own_masks[A]).astype(low),
        ((middle_b + z_sum(*final_b)) * own_masks[B]).astype(low),
    ]
    token_grad_a = norm_ones[A][1](first_sum[A])[0]
    token_grad_b = norm_ones[B][1](first_sum[B])[0]
    mixer_gain_grad = (
        jnp.sum(part3_a * first_a.astype(wide), axis=0)
        + jnp.sum(part3_b * first_b.astype(wide), axis=0)
    ) / mixer_gain
    input_grads = [middle_grad_a + token_grad_a, middle_grad_b + token_grad_b]
    feed_gain_grad = gain_grad_a + gain_grad_b
    conv_grads, rate_grads, gain_grads = [x + y for x, y in zip(core_a, core_b)]
    rate_grads, gain_grads = rate_grads[:2, :head_count], gain_grads[0]
    everywhere = jnp.concatenate([feed_gain_grad, mixer_gain_grad, gain_grads])
    per_slice = jnp.concatenate([conv_grads.reshape(-1), rate_grads.reshape(-1)])
    packed = sum_over(jnp.concatenate([per_slice, everywhere]), "dp")
    slices = jnp.zeros((tensor_count, per_slice.size), wide)
    slices = lax.dynamic_update_index_in_dim(slices, packed[: per_slice.size], tensor_index, 0)
    packed = sum_over(jnp.concatenate([slices.reshape(-1), packed[per_slice.size :]]), "tensor")
    slices = packed[: slices.size].reshape(tensor_count, per_slice.size)
    taps = query_conv.shape[0]
    conv_all = slices[:, : conv_grads.size].reshape(tensor_count, taps, -1)

    def all_columns(begin, end):
        return jnp.moveaxis(conv_all[:, :, begin:end], 0, 1).reshape(taps, -1)

    rate_all = slices[:, conv_grads.size :]
    everywhere = packed[slices.size :]
    return (
        jnp.stack(outputs),
        jnp.stack(input_grads),
        everywhere[width : 2 * width],
        in_final[:, : edges[0]],
        in_final[:, edges[0] : edges[1]],
        in_final[:, edges[1] : edges[2]],
        in_final[:, edges[2] : edges[3]],
        in_final[:, edges[3] : edges[3] + head_count],
        in_final[:, edges[3] + head_count : edges[3] + 2 * head_count],
        all_columns(0, edges[0]),
        all_columns(edges[0], edges[1]),
        all_columns(edges[1], edges[2]),
        rate_all[:, :head_count].reshape(-1),
        rate_all[:, head_count:].reshape(-1),
        everywhere[2 * width :],
        out_final.T,
        everywhere[:width],
        both_final[:, :hidden_width],
        both_final[:, hidden_width:feed_width],
        both_final[:, feed_width:].T,
    )


def solution(mesh):
    return jax.shard_map(
        shards,
        mesh=mesh,
        in_specs=(
            P(None, ("dp", "tensor"), None),
            P(None, "dp", None),
            P(),
            P("dp", "tensor"),
            P("dp", "tensor"),
            P("dp", "tensor"),
            P("dp", "tensor"),
            P("dp", "tensor"),
            P("dp", "tensor"),
            P(),
            P(),
            P(),
            P(),
            P(),
            P(),
            P("tensor", "dp"),
            P(),
            P("dp", "tensor"),
            P("dp", "tensor"),
            P("tensor", "dp"),
            P(None, ("dp", "tensor"), None),
        ),
        out_specs=(
            P(None, ("dp", "tensor"), None),
            P(None, ("dp", "tensor"), None),
            P(),
            P("dp", "tensor"),
            P("dp", "tensor"),
            P("dp", "tensor"),
            P("dp", "tensor"),
            P("dp", "tensor"),
            P("dp", "tensor"),
            P(),
            P(),
            P(),
            P(),
            P(),
            P(),
            P("tensor", "dp"),
            P(),
            P("dp", "tensor"),
            P("dp", "tensor"),
            P("tensor", "dp"),
        ),
        check_vma=False,
    )
```
